256 devices in a mesh: tile: 64 (over y, x, z_lo), rep: 4 (over z_hi, core).
Axes of the slice: x: 4, y: 4, z: 8 (z_hi: 2, z_lo: 4; z = z_hi * 4 + z_lo), core: 2. Of those that a mesh axis runs over, the one named last changes fastest.
Arguments:
- inputs: bfloat16 [65536, 1024], P(('rep', 'tile')), parts along dimension 0, may hold values from -6 to 6
- queries: bfloat16 [65536, 1024], P(('rep', 'tile')), parts along dimension 0, may hold values from -180 to 180
- key_vectors: bfloat16 [65536, 1024], P(('rep', 'tile')), parts along dimension 0, may hold values from -6 to 6
- values: bfloat16 [65536, 1024], P(('rep', 'tile')), parts along dimension 0, may hold values from -16 to 16
- out_weight: bfloat16 [1024, 1024], replicated, may hold values from -0.1875 to 0.1875
- norm_gain: float32 [1024], replicated, may hold values from 0.5 to 1.5
- routes: int32 [65536, 2], P(('rep', 'tile')), parts along dimension 0, may hold values from 0 to 63, all different within a row; in each aligned block of 128 rows (0 to 127, 128 to 255, ...) at most 8 rows name the same one
- route_gates: float32 [65536, 2], P(('rep', 'tile')), parts along dimension 0, may hold values from 0.2 to 1
- w_gate: bfloat16 [64, 1024, 1408], P('tile'), may hold values from -0.1875 to 0.1875
- w_up: bfloat16 [64, 1024, 1408], P('tile'), may hold values from -0.1875 to 0.1875
- w_down: bfloat16 [64, 1408, 1024], P('tile'), may hold values from -0.15625 to 0.15625
Outputs:
- layer_out: bfloat16 [65536, 1024], P(('rep', 'tile')), parts along dimension 0
The draws below stay inside these ranges and needn't reach their ends.
There are 4 independent parts, one for each index of `rep`. The reference program is written for one: setup_inputs(seed, part) draws one part's arguments, and reference() takes and returns one part's arrays. A program takes and returns all parts, laid end to end along the dimension named above; an argument that names none is the same for every part. Nothing has to cross between parts.
Inputs may be any that keep to these rules, and one draw needn't show every extreme that they name: `routes`: in each aligned block of 128 tokens no expert is named by more than 8 tokens, and some expert is named by exactly that many; each token names 2 different experts.
All inputs are finite; a program needn't handle non-finite values.
Results may differ from the reference program's by a relative error of at most 0.0061.
Values may be sent and summed in bfloat16 or wider, within the bound.
A program may use at most 64 MiB of HBM per device.

```python
import math
import jax
import jax.numpy as jnp
import numpy as np
from jax import lax

D = 1024
HEADS = 16
HD = 64
H = 1408
TOPK = 2
IL_DEV = 4
XL = 8
DP = 8
R_IL = 2
R_XL = 2
R_DP = 2
TOK_DEV = 256
TOKENS = 16384
NIL = 256
EXPERTS = 64
CAP_HALF = 8
N_TILE = 64


def key_table(key):
    raw = jax.random.normal(jax.random.fold_in(key, 11), (TOKENS, D), jnp.float32)
    return jnp.clip(raw, -6.0, 6.0)


def draw_key_vectors(key, part):
    base_keys = key_table(key)
    return base_keys.astype(jnp.bfloat16)


def draw_queries(key, part):
    raw = jax.random.normal(jax.random.fold_in(key, 12), (TOKENS, D), jnp.float32)
    raw = jnp.clip(raw, -6.0, 6.0)
    return raw.astype(jnp.bfloat16)


def shard_levels(own_key, dims, shards, low, largest):
    level = 1.0
    for axis_at, blocks in shards:
        steps = jax.random.uniform(jax.random.fold_in(jax.random.fold_in(own_key, 6), axis_at), (blocks,), jnp.float32, low / len(shards), largest / len(shards))
        level = level * jnp.repeat(jnp.exp(steps), dims[axis_at] // blocks).reshape((-1,) + (1,) * (len(dims) - 1 - axis_at))
    return level


def assign_block(rng, own, number, rows, count, top, reach, lean):
    sequence = jax.random.permutation(rng, count)
    crowded, common = shares(count, rows * top, reach, lean, True), shares(count, rows * top, reach, lean, False)
    places = jnp.arange(count)

    def named(tallies, turn):
        used = int((tallies > 0).sum())
        fixed = max(1, used // 4)
        moved = fixed + (places - fixed + turn * (used - fixed)) % max(1, count - fixed)
        return jnp.zeros((count,), jnp.int32).at[sequence[jnp.where(places < fixed, places, moved)]].set(jnp.asarray(tallies, jnp.int32))

    tallies = jnp.where(number % 4 == 0, named(crowded, number // 4), named(common, number - number // 4 - 1))
    mixed = jax.random.permutation(jax.random.fold_in(own, 3), count)
    source_of, sink = mixed[0:count // 2 * 2:2], mixed[1:count // 2 * 2:2]
    slack = jnp.minimum(tallies[source_of] - 1, reach - tallies[sink]) // 2
    slack = jnp.where((source_of == sequence[0]) | (sink == sequence[0]) | (tallies[sink] == 0), 0, jnp.maximum(slack, 0))
    moved = jax.random.randint(jax.random.fold_in(own, 4), (count // 2,), 0, 1 << 20) % (slack + 1)
    tallies = tallies.at[source_of].add(-moved).at[sink].add(moved)
    members = jnp.searchsorted(jnp.cumsum(tallies), jnp.arange(rows * top), side="right").astype(jnp.int32)
    grid = members.reshape(top, rows).T
    grid = grid[jax.random.permutation(jax.random.fold_in(own, 1), rows)]
    turn = jax.random.randint(jax.random.fold_in(own, 2), (rows, 1), 0, top)
    return jnp.take_along_axis(grid, (jnp.arange(top)[None, :] + turn) % top, axis=1)


def shares(amount, total, bound, slope, full):
    weights = [(1 << 20) // math.isqrt(rank ** slope) + 1 for rank in range(1, amount + 1)]
    largest = bound if full else min(bound, max(-(-total // amount), total * weights[0] // sum(weights)))
    least = 1 if total - largest >= amount - 1 else 0
    holding, rest = [largest] + [least] * (amount - 1), total - largest - least * (amount - 1)
    while rest > 0:
        movable = [i for i in range(1, amount) if holding[i] < largest] or [i for i in range(1, amount) if holding[i] < bound]
        mass, left = sum([weights[i] for i in movable]), rest
        for i in movable:
            more = min(bound - holding[i], max(1, left * weights[i] // mass), rest)
            holding[i] = holding[i] + more
            rest = rest - more
    return np.array(holding)


def normal_values(stream_key, shape, scale, bound, shards=(), held_as=jnp.bfloat16):
    factor_of = shard_levels(stream_key, shape, shards, -0.22, 0.18) if shards else 1.0
    values = jax.random.normal(stream_key, shape, jnp.float32) * scale * factor_of
    return jnp.minimum(jnp.maximum(values, -bound), bound).astype(held_as)


def setup_inputs(seed: int = 0, part: int = 0) -> dict:
    seeds = jax.random.split(jax.random.key(seed), 12)
    own_keys = jax.random.split(jax.random.fold_in(seeds[11], part), 12)
    inputs = normal_values(own_keys[0], (TOKENS, D), 1.0, 6.0, ((0, 64),))
    queries = draw_queries(jax.random.fold_in(jax.random.fold_in(seeds[11], part), 71), part)
    key_vectors = draw_key_vectors(jax.random.fold_in(jax.random.fold_in(seeds[11], part), 71), part)
    values = normal_values(own_keys[3], (TOKENS, D), 3.0, 16.0, ((0, 64),))
    out_weight = normal_values(seeds[4], (D, D), D ** -0.5, 0.1875)
    norm_gain = jnp.clip(1.0 + 0.1 * jax.random.normal(seeds[5], (D,), jnp.float32), 0.5, 1.5)
    routes_keys = jax.random.split(jax.random.fold_in(own_keys[6], 1), TOKENS // (TOK_DEV // 2))
    routes_turns = jax.random.permutation(jax.random.fold_in(own_keys[6], 3), TOKENS // (TOK_DEV // 2))
    routes = jax.vmap(lambda own, number: assign_block(jax.random.fold_in(own_keys[6], 2), own, number, TOK_DEV // 2, EXPERTS, TOPK, CAP_HALF, 2))(routes_keys, routes_turns).reshape((TOKENS, TOPK))
    route_gates = jnp.clip(0.2 + 0.8 * jax.random.uniform(own_keys[7], (TOKENS, TOPK), jnp.float32) ** shard_levels(own_keys[7], (TOKENS, TOPK), ((0, 64),), -0.2, 0.2), 0.2, 1.0)
    w_gate = normal_values(seeds[8], (EXPERTS, D, H), D ** -0.5, 0.1875, ((0, 64),))
    w_up = normal_values(seeds[9], (EXPERTS, D, H), D ** -0.5, 0.1875, ((0, 64),))
    w_down = normal_values(seeds[10], (EXPERTS, H, D), H ** -0.5, 0.15625, ((0, 64),))
    return {"inputs": inputs, "queries": queries, "key_vectors": key_vectors, "values": values, "out_weight": out_weight, "norm_gain": norm_gain, "routes": routes, "route_gates": route_gates, "w_gate": w_gate, "w_up": w_up, "w_down": w_down}


def local_attention(query_block, key_block, value_block, first_inline, total_inlines):
    query_count = query_block.shape[0]
    key_count = key_block.shape[0]
    plane = XL * DP
    query_pos = jnp.arange(query_count, dtype=jnp.int32)
    key_pos = jnp.arange(key_count, dtype=jnp.int32)
    query_il = query_pos // plane
    query_xl = query_pos // DP % XL
    query_dp = query_pos % DP
    key_il = key_pos // plane - R_IL
    key_xl = key_pos // DP % XL
    key_dp = key_pos % DP
    near = jnp.abs(query_il[:, None] - key_il[None, :]) <= R_IL
    near = near & (jnp.abs(query_xl[:, None] - key_xl[None, :]) <= R_XL)
    near = near & (jnp.abs(query_dp[:, None] - key_dp[None, :]) <= R_DP)
    inside = (first_inline + key_il >= 0) & (first_inline + key_il < total_inlines)
    near = near & inside[None, :]
    query_heads = query_block.reshape(query_count, HEADS, HD).astype(jnp.float32)
    key_heads = key_block.reshape(key_count, HEADS, HD).astype(jnp.float32)
    value_heads = value_block.reshape(key_count, HEADS, HD).astype(jnp.float32)
    scores = jnp.einsum('qhd,khd->hqk', query_heads, key_heads) * (1.0 / HD ** 0.5)
    scores = jnp.where(near[None], scores, jnp.float32(-1e+30))
    highest = lax.optimization_barrier(jnp.max(scores, axis=-1, keepdims=True))
    weights = jnp.exp(scores - highest)
    weights = jnp.where(near[None], weights, jnp.float32(0.0))
    totals = lax.optimization_barrier(jnp.sum(weights, axis=-1, keepdims=True))
    probs = (weights / totals).astype(jnp.bfloat16)
    attended = jnp.einsum('hqk,khd->qhd', probs.astype(jnp.float32), value_heads)
    return attended.astype(jnp.bfloat16).reshape(query_count, HEADS * HD)

def expert_rows(token_rows, gate_mat, up_mat, down_mat):
    gate_part = jnp.dot(token_rows, gate_mat, preferred_element_type=jnp.float32)
    up_part = jnp.dot(token_rows, up_mat, preferred_element_type=jnp.float32)
    hidden = (jax.nn.silu(gate_part) * up_part).astype(jnp.bfloat16)
    return jnp.dot(hidden, down_mat, preferred_element_type=jnp.float32).astype(jnp.bfloat16)

def slot_ranks(routes, experts, block_rows):
    row_count = routes.shape[0]
    expert_ids = jnp.arange(experts, dtype=jnp.int32)
    matches = routes[:, :, None] == expert_ids[None, None, :]
    hits = lax.optimization_barrier(jnp.sum(matches.astype(jnp.int32), axis=1))
    hits = hits.reshape(row_count // block_rows, block_rows, experts)
    earlier = (jnp.cumsum(hits, axis=1) - hits).reshape(row_count, experts)
    return lax.optimization_barrier(jnp.sum(jnp.where(matches, earlier[:, None, :], 0), axis=-1)).astype(jnp.int32)

def reference(inputs, queries, key_vectors, values, out_weight, norm_gain, routes, route_gates, w_gate, w_up, w_down):
    width = R_IL * XL * DP
    zero_rows = jnp.zeros((width, D), jnp.bfloat16)
    padded_keys = jnp.concatenate([zero_rows, key_vectors, zero_rows], axis=0)
    padded_values = jnp.concatenate([zero_rows, values, zero_rows], axis=0)

    def one_tile(tile_id):
        start = (tile_id * TOK_DEV).astype(jnp.int32)
        query_block = lax.dynamic_slice_in_dim(queries, start, TOK_DEV, 0)
        key_block = lax.dynamic_slice_in_dim(padded_keys, start, TOK_DEV + 2 * width, 0)
        value_block = lax.dynamic_slice_in_dim(padded_values, start, TOK_DEV + 2 * width, 0)
        return local_attention(query_block, key_block, value_block, (tile_id * IL_DEV).astype(jnp.int32), NIL)
    attended = lax.map(one_tile, jnp.arange(N_TILE, dtype=jnp.int32)).reshape(TOKENS, D)
    residual = (inputs.astype(jnp.float32) + jnp.dot(attended, out_weight, preferred_element_type=jnp.float32)).astype(jnp.bfloat16)
    resid_float = residual.astype(jnp.float32)
    mean_square = lax.optimization_barrier(jnp.mean(resid_float * resid_float, axis=-1, keepdims=True))
    normed = (resid_float * lax.rsqrt(mean_square + 1e-06) * norm_gain[None, :]).astype(jnp.bfloat16)
    block_rows = TOK_DEV // 2
    slot_rank = slot_ranks(routes, EXPERTS, block_rows)
    token_ids = jnp.arange(TOKENS, dtype=jnp.int32)
    source = (token_ids // TOK_DEV)[:, None]
    half_index = (token_ids // block_rows % 2)[:, None]
    positions = (source * (2 * CAP_HALF) + half_index * CAP_HALF + slot_rank).astype(jnp.int32)
    buffer_rows = N_TILE * 2 * CAP_HALF
    owners = jnp.full((EXPERTS, buffer_rows), TOKENS, jnp.int32)
    owners = owners.at[routes, positions].set(jnp.broadcast_to(token_ids[:, None], routes.shape))
    normed_padded = jnp.concatenate([normed, jnp.zeros((1, D), jnp.bfloat16)], axis=0)

    def one_expert(expert_id):
        picked_rows = normed_padded[owners[expert_id]]
        return expert_rows(picked_rows, w_gate[expert_id], w_up[expert_id], w_down[expert_id])
    outputs = lax.map(one_expert, jnp.arange(EXPERTS, dtype=jnp.int32))
    picked = outputs[routes, positions].astype(jnp.float32)
    combined = lax.optimization_barrier(jnp.sum(route_gates[:, :, None] * picked, axis=1))
    return (resid_float + combined).astype(jnp.bfloat16)
```

```python
import jax
import jax.numpy as jnp
from jax import lax
from jax.experimental import pallas as pl
from jax.experimental.pallas import tpu as pltpu
from jax.sharding import PartitionSpec as P

HEADS = 16
HD = 64
IL_DEV = 4
XL = 8
DP = 8
R_IL = 2
R_XL = 2
R_DP = 2
ZN = 4
JN = 16
CAP = 16
MESH = pl.DeviceIdType.MESH


def with_halo(shard, sides, width):
    for axis, dim in sides:
        count, length = (lax.axis_size(axis), shard.shape[dim])
        up = [(i, (i + 1) % count) for i in range(count - 1)]
        down = [(j, i) for i, j in up]
        last = lax.slice_in_dim(shard, length - width, length, axis=dim)
        initial = lax.slice_in_dim(shard, 0, width, axis=dim)
        before = lax.ppermute(last, axis, up)
        after = lax.ppermute(initial, axis, down)
        shard = jnp.concatenate([before, shard, after], axis=dim)
    return shard


def local_attention(query_block, key_block, value_block, first_inline, total_inlines):
    query_count = query_block.shape[0]
    key_count = key_block.shape[0]
    plane = XL * DP
    query_pos = jnp.arange(query_count, dtype=jnp.int32)
    key_pos = jnp.arange(key_count, dtype=jnp.int32)
    query_il = query_pos // plane
    query_xl = query_pos // DP % XL
    query_dp = query_pos % DP
    key_il = key_pos // plane - R_IL
    key_xl = key_pos // DP % XL
    key_dp = key_pos % DP
    near = jnp.abs(query_il[:, None] - key_il[None, :]) <= R_IL
    near = near & (jnp.abs(query_xl[:, None] - key_xl[None, :]) <= R_XL)
    near = near & (jnp.abs(query_dp[:, None] - key_dp[None, :]) <= R_DP)
    inside = (first_inline + key_il >= 0) & (first_inline + key_il < total_inlines)
    near = near & inside[None, :]
    query_heads = query_block.reshape(query_count, HEADS, HD)
    key_heads = key_block.reshape(key_count, HEADS, HD)
    value_heads = value_block.reshape(key_count, HEADS, HD)
    scores = jnp.einsum(
        "qhd,khd->hqk", query_heads, key_heads, preferred_element_type=jnp.float32
    ) * (1.0 / HD**0.5)
    scores = jnp.where(near[None], scores, jnp.float32(-1e30))
    highest = jnp.max(scores, axis=-1, keepdims=True)
    weights = jnp.exp(scores - highest)
    weights = jnp.where(near[None], weights, jnp.float32(0.0))
    totals = jnp.sum(weights, axis=-1, keepdims=True)
    probs = (weights / totals).astype(jnp.bfloat16)
    attended = jnp.einsum("hqk,khd->qhd", probs, value_heads, preferred_element_type=jnp.float32)
    return attended.astype(jnp.bfloat16).reshape(query_count, HEADS * HD)


def slot_ranks(routes, experts, block_rows):
    row_count = routes.shape[0]
    expert_ids = jnp.arange(experts, dtype=jnp.int32)
    matches = routes[:, :, None] == expert_ids[None, None, :]
    hits = jnp.sum(matches.astype(jnp.int32), axis=1)
    hits = hits.reshape(row_count // block_rows, block_rows, experts)
    earlier = (jnp.cumsum(hits, axis=1) - hits).reshape(row_count, experts)
    return jnp.sum(jnp.where(matches, earlier[:, None, :], 0), axis=-1)


def tile_order(z, it):
    low = jnp.where(z == 0, it, lax.rem(it + 1, ZN))
    mirrored = jnp.where(z == 3, it, lax.rem(it + 1, ZN))
    return jnp.where(z < 2, low, 3 - mirrored)


def moe_kernel(
    x_ref,
    res_ref,
    meta_ref,
    wg_hbm,
    wu_hbm,
    wd_hbm,
    out_ref,
    wg,
    wu,
    wd,
    meta_all,
    x_all,
    disp,
    recv,
    eout,
    ret,
    own,
    rs_out,
    rs_in,
    w_sem,
    meta_send,
    meta_recv,
    ag_send,
    fw_send,
    ag_recv,
    xs,
    xr,
    ys,
    yr,
    rs_send,
    rs_recv,
):
    t = lax.axis_index("tile")
    z = lax.rem(t, ZN)
    j = lax.div(t, ZN)
    rows = x_ref.shape[0]
    model = x_ref.shape[1]

    w_copies = [
        pltpu.make_async_copy(wg_hbm.at[0], wg, w_sem.at[0]),
        pltpu.make_async_copy(wu_hbm.at[0], wu, w_sem.at[1]),
        pltpu.make_async_copy(wd_hbm.at[0], wd, w_sem.at[2]),
    ]

    barrier = pltpu.get_barrier_semaphore()

    def z_peer(d):
        return j * ZN + lax.rem(z + d, ZN)

    def plane_peer(d):
        return lax.rem(j + d, JN)

    def greet_plane(d, carry):
        pl.semaphore_signal(
            barrier, inc=1, device_id={"tile": plane_peer(d) * ZN + z}, device_id_type=MESH
        )
        return carry

    lax.fori_loop(1, JN, greet_plane, 0)
    for d in range(1, ZN):
        pl.semaphore_signal(barrier, inc=1, device_id={"tile": z_peer(d)}, device_id_type=MESH)
    for c in w_copies:
        c.start()
    pl.semaphore_wait(barrier, JN - 1 + ZN - 1)

    def send_tile(src, slot, to, send_sem):
        return pltpu.make_async_remote_copy(
            src_ref=src,
            dst_ref=x_all.at[slot],
            send_sem=send_sem,
            recv_sem=ag_recv.at[slot],
            device_id={"tile": to},
            device_id_type=MESH,
        )

    def send_meta(d):
        return pltpu.make_async_remote_copy(
            src_ref=meta_ref,
            dst_ref=meta_all.at[z],
            send_sem=meta_send.at[d - 1],
            recv_sem=meta_recv.at[z],
            device_id={"tile": z_peer(d)},
            device_id_type=MESH,
        )

    for d in range(1, ZN):
        send_meta(d).start()

    @pl.when(z < ZN - 1)
    def _():
        send_tile(x_ref, z, t + 1, ag_send.at[0]).start()

    @pl.when(z > 0)
    def _():
        send_tile(x_ref, z, t - 1, ag_send.at[1]).start()

    meta_all[z] = meta_ref[...]
    x_all[z] = x_ref[...]

    def tile_arrived(slot):
        send_tile(x_ref, slot, t, ag_send.at[0]).wait_recv()

    def arrive(distance):
        @pl.when(z - distance >= 0)
        def _():
            tile_arrived(z - distance)

            @pl.when(z + 1 < ZN)
            def _():
                send_tile(x_all.at[z - distance], z - distance, t + 1, fw_send.at[z - distance]).start()

        @pl.when(z + distance < ZN)
        def _():
            tile_arrived(z + distance)

            @pl.when(z - 1 >= 0)
            def _():
                send_tile(x_all.at[z + distance], z + distance, t - 1, fw_send.at[z + distance]).start()

    def dispatch_copy(it, d):
        return pltpu.make_async_remote_copy(
            src_ref=disp.at[it, plane_peer(d)],
            dst_ref=recv.at[it, j],
            send_sem=xs.at[it],
            recv_sem=xr.at[it],
            device_id={"tile": plane_peer(d) * ZN + z},
            device_id_type=MESH,
        )

    def return_copy(it, d):
        return pltpu.make_async_remote_copy(
            src_ref=eout.at[it, plane_peer(d)],
            dst_ref=ret.at[it, j],
            send_sem=ys.at[it],
            recv_sem=yr.at[it],
            device_id={"tile": plane_peer(d) * ZN + z},
            device_id_type=MESH,
        )

    def all_of(src, dst, it, send_sem, recv_sem):
        return pltpu.make_async_remote_copy(
            src_ref=src.at[it, pl.ds(0, JN - 1)],
            dst_ref=dst.at[it, pl.ds(0, JN - 1)],
            send_sem=send_sem.at[it],
            recv_sem=recv_sem.at[it],
            device_id={"tile": t},
            device_id_type=MESH,
        )

    slots = JN * CAP
    slot_of = lax.broadcasted_iota(jnp.int32, (slots, rows), 0).astype(jnp.float32)

    def stage_dispatch(it):
        for distance in range(1, ZN):

            @pl.when(it == distance)
            def _():
                arrive(distance)

        s = tile_order(z, it)
        base = (z * slots).astype(jnp.float32)
        meta = meta_all[s] - base
        picks = (slot_of == meta[0:1]) | (slot_of == meta[1:2])
        table = picks.astype(jnp.float32).astype(jnp.bfloat16)
        picked = jnp.dot(table, x_all[s], preferred_element_type=jnp.float32).astype(jnp.bfloat16)
        disp[it] = picked.reshape(JN, CAP, model)

        def start(d, carry):
            dispatch_copy(it, d).start()
            return carry

        lax.fori_loop(1, JN, start, 0)
        recv[it, j] = disp[it, j]

    def stage_expert(it):
        all_of(disp, recv, it, xs, xr).wait_recv()
        zrows = recv[it].reshape(slots, model)
        gate_part = jnp.dot(zrows, wg[...], preferred_element_type=jnp.float32)
        up_part = jnp.dot(zrows, wu[...], preferred_element_type=jnp.float32)
        hidden = (gate_part / (1.0 + jnp.exp(-gate_part)) * up_part).astype(jnp.bfloat16)
        result = jnp.dot(hidden, wd[...], preferred_element_type=jnp.float32)
        eout[it] = result.astype(jnp.bfloat16).reshape(JN, CAP, model)

        def start(d, carry):
            return_copy(it, d).start()
            return carry

        lax.fori_loop(1, JN, start, 0)
        ret[it, j] = eout[it, j]

    def rs_copy(it):
        s = tile_order(z, it)
        return pltpu.make_async_remote_copy(
            src_ref=rs_out.at[it],
            dst_ref=rs_in.at[z],
            send_sem=rs_send.at[it],
            recv_sem=rs_recv.at[z],
            device_id={"tile": j * ZN + s},
            device_id_type=MESH,
        )

    def stage_combine(it):
        all_of(eout, ret, it, ys, yr).wait_recv()
        s = tile_order(z, it)
        base = (z * slots).astype(jnp.float32)
        meta = meta_all[s]
        pos = meta[0:2] - base
        weights = jnp.where(slot_of == pos[0:1], meta[2:3], 0.0) + jnp.where(
            slot_of == pos[1:2], meta[3:4], 0.0
        )
        part = lax.dot_general(
            weights.astype(jnp.bfloat16),
            ret[it].reshape(slots, model),
            (((0,), (0,)), ((), ())),
            preferred_element_type=jnp.float32,
        )

        @pl.when(it == 0)
        def _():
            own[...] = part

        @pl.when(it > 0)
        def _():
            rs_out[it] = part.astype(jnp.bfloat16)
            rs_copy(it).start()

    def step(it, carry):
        @pl.when(it == 0)
        def _():
            for d in range(1, ZN):
                src = lax.rem(z + d, ZN)
                pltpu.make_async_remote_copy(
                    src_ref=meta_ref,
                    dst_ref=meta_all.at[src],
                    send_sem=meta_send.at[0],
                    recv_sem=meta_recv.at[src],
                    device_id={"tile": t},
                    device_id_type=MESH,
                ).wait_recv()
            for c in w_copies:
                c.wait()

        @pl.when(it < ZN)
        def _():
            stage_dispatch(it)

        @pl.when(it > 0)
        def _():
            stage_combine(it - 1)

        @pl.when(it < ZN)
        def _():
            stage_expert(it)

        return carry

    lax.fori_loop(0, ZN + 1, step, 0)

    total = own[...] + res_ref[...].astype(jnp.float32)
    for d in range(1, ZN):
        src = lax.rem(z + d, ZN)
        pltpu.make_async_remote_copy(
            src_ref=rs_out.at[0],
            dst_ref=rs_in.at[src],
            send_sem=rs_send.at[0],
            recv_sem=rs_recv.at[src],
            device_id={"tile": t},
            device_id_type=MESH,
        ).wait_recv()
        total = total + rs_in[src].astype(jnp.float32)
    out_ref[...] = total.astype(jnp.bfloat16)

    for d in range(1, ZN):
        send_meta(d).wait_send()

    @pl.when(z < ZN - 1)
    def _():
        send_tile(x_ref, z, t + 1, ag_send.at[0]).wait_send()

    @pl.when(z > 0)
    def _():
        send_tile(x_ref, z, t - 1, ag_send.at[1]).wait_send()

    for distance in range(1, ZN):

        @pl.when((z - distance >= 0) & (z + 1 < ZN))
        def _():
            send_tile(x_all.at[z - distance], z - distance, t, fw_send.at[z - distance]).wait_send()

        @pl.when((z + distance < ZN) & (z - 1 >= 0))
        def _():
            send_tile(x_all.at[z + distance], z + distance, t, fw_send.at[z + distance]).wait_send()

    def drain(it, carry):
        all_of(disp, recv, it, xs, xr).wait_send()
        all_of(eout, ret, it, ys, yr).wait_send()

        @pl.when(it > 0)
        def _():
            rs_copy(it).wait_send()

        return carry

    lax.fori_loop(0, ZN, drain, 0)


def routed_experts(normed, residual, meta, w_gate, w_up, w_down):
    rows, model = normed.shape
    wide = w_gate.shape[2]
    bf16 = jnp.bfloat16
    vmem = pl.BlockSpec(memory_space=pltpu.VMEM)
    anywhere = pl.BlockSpec(memory_space=pl.ANY)
    dma = pltpu.SemaphoreType.DMA
    return pl.pallas_call(
        moe_kernel,
        out_shape=jax.ShapeDtypeStruct((rows, model), bf16),
        in_specs=[vmem, vmem, vmem, anywhere, anywhere, anywhere],
        out_specs=vmem,
        scratch_shapes=[
            pltpu.VMEM((model, wide), bf16),
            pltpu.VMEM((model, wide), bf16),
            pltpu.VMEM((wide, model), bf16),
            pltpu.VMEM((ZN, 8, rows), jnp.float32),
            pltpu.VMEM((ZN, rows, model), bf16),
            pltpu.VMEM((ZN, JN, CAP, model), bf16),
            pltpu.VMEM((ZN, JN, CAP, model), bf16),
            pltpu.VMEM((ZN, JN, CAP, model), bf16),
            pltpu.VMEM((ZN, JN, CAP, model), bf16),
            pltpu.VMEM((rows, model), jnp.float32),
            pltpu.VMEM((ZN, rows, model), bf16),
            pltpu.VMEM((ZN, rows, model), bf16),
            dma((3,)),
            dma((3,)),
            dma((ZN,)),
            dma((2,)),
            dma((ZN,)),
            dma((ZN,)),
            dma((ZN,)),
            dma((ZN,)),
            dma((ZN,)),
            dma((ZN,)),
            dma((ZN,)),
            dma((ZN,)),
        ],
        compiler_params=pltpu.CompilerParams(
            collective_id=1, has_side_effects=True, vmem_limit_bytes=56 * 1024 * 1024
        ),
    )(normed, residual, meta, w_gate, w_up, w_down)


def local(
    inputs,
    queries,
    key_vectors,
    values,
    out_weight,
    norm_gain,
    routes,
    route_gates,
    w_gate,
    w_up,
    w_down,
):
    row_count = inputs.shape[0]
    model = inputs.shape[1]
    tiles = lax.axis_size("tile")
    first_inline = lax.axis_index("tile") * IL_DEV
    width = R_IL * XL * DP
    key_value = jnp.concatenate([key_vectors, values], axis=1)
    extended = with_halo(key_value, (("tile", 0),), width)
    attended = local_attention(
        queries, extended[:, :model], extended[:, model:], first_inline, IL_DEV * tiles
    )
    residual = (
        inputs.astype(jnp.float32)
        + jnp.dot(attended, out_weight, preferred_element_type=jnp.float32)
    ).astype(jnp.bfloat16)
    resid_float = residual.astype(jnp.float32)
    mean_square = jnp.mean(resid_float * resid_float, axis=-1, keepdims=True)
    normed = (resid_float * lax.rsqrt(mean_square + 1e-06) * norm_gain[None, :]).astype(
        jnp.bfloat16
    )
    block_rows = row_count // 2
    slot_rank = slot_ranks(routes, tiles, block_rows)
    half_index = (jnp.arange(row_count, dtype=jnp.int32) // block_rows)[:, None]
    pos = (
        routes % ZN * (JN * CAP) + routes // ZN * CAP + half_index * (CAP // 2) + slot_rank
    ).astype(jnp.float32)
    meta = jnp.concatenate([pos.T, route_gates.T, jnp.zeros((4, row_count), jnp.float32)], axis=0)
    return routed_experts(normed, residual, meta, w_gate, w_up, w_down)


def solution(mesh):
    return jax.shard_map(
        local,
        mesh=mesh,
        in_specs=(
            P(("rep", "tile"), None),
            P(("rep", "tile"), None),
            P(("rep", "tile"), None),
            P(("rep", "tile"), None),
            P(),
            P(),
            P(("rep", "tile"), None),
            P(("rep", "tile"), None),
            P("tile", None, None),
            P("tile", None, None),
            P("tile", None, None),
        ),
        out_specs=P(("rep", "tile"), None),
        check_vma=False,
    )
```

```python
import jax
import jax.numpy as jnp
from jax import lax
from jax.experimental import pallas as pl
from jax.experimental.pallas import tpu as pltpu
from jax.sharding import PartitionSpec as P

HEADS = 16
HD = 64
IL_DEV = 4
XL = 8
DP = 8
R_IL = 2
R_XL = 2
R_DP = 2
ZN = 4
JN = 16
CAP = 16
MESH = pl.DeviceIdType.MESH


def tile_order(z, it):
    low = jnp.where(z == 0, it, lax.rem(it + 1, ZN))
    mirrored = jnp.where(z == 3, it, lax.rem(it + 1, ZN))
    return jnp.where(z < 2, low, 3 - mirrored)


def layer_kernel(
    x_hbm,
    q_hbm,
    k_hbm,
    v_hbm,
    ow_hbm,
    gain_ref,
    routes_ref,
    gates_ref,
    wg_hbm,
    wu_hbm,
    wd_hbm,
    out_ref,
    x_in,
    q_in,
    ke,
    ve,
    ow,
    att,
    near,
    wg,
    wu,
    wd,
    meta_own,
    meta_all,
    x_all,
    resid,
    disp,
    recv,
    eout,
    ret,
    own,
    rs_out,
    rs_in,
    l_sem,
    h_send,
    h_recv,
    meta_send,
    meta_recv,
    ag_send,
    fw_send,
    ag_recv,
    xs,
    xr,
    ys,
    yr,
    rs_send,
    rs_recv,
):
    t = lax.axis_index("tile")
    tiles = lax.axis_size("tile")
    z = lax.rem(t, ZN)
    j = lax.div(t, ZN)
    rows = x_in.shape[0]
    model = x_in.shape[1]
    plane = XL * DP
    halo = R_IL * plane
    keys = (2 * R_IL + 1) * plane
    bf16 = jnp.bfloat16
    f32 = jnp.float32

    def local_copy(src, dst, n):
        return pltpu.make_async_copy(src, dst, l_sem.at[n])

    early = [
        local_copy(k_hbm, ke.at[pl.ds(halo, rows)], 0),
        local_copy(v_hbm, ve.at[pl.ds(halo, rows)], 1),
        local_copy(q_hbm, q_in, 2),
    ]
    mid = [local_copy(x_hbm, x_in, 3), local_copy(ow_hbm, ow, 4)]
    late = [
        local_copy(wg_hbm.at[0], wg, 5),
        local_copy(wu_hbm.at[0], wu, 6),
        local_copy(wd_hbm.at[0], wd, 7),
    ]

    barrier = pltpu.get_barrier_semaphore()

    def greet(tile):
        pl.semaphore_signal(barrier, inc=1, device_id={"tile": tile}, device_id_type=MESH)

    def z_peer(d):
        return j * ZN + lax.rem(z + d, ZN)

    def plane_peer(d):
        return lax.rem(j + d, JN)

    @pl.when(t > 0)
    def _():
        greet(t - 1)

    @pl.when(t < tiles - 1)
    def _():
        greet(t + 1)

    for d in range(1, ZN):
        greet(z_peer(d))

    def greet_plane(d, carry):
        greet(plane_peer(d) * ZN + z)
        return carry

    lax.fori_loop(1, JN, greet_plane, 0)
    for c in early + mid + late:
        c.start()
    pl.semaphore_wait(
        barrier,
        JN - 1 + ZN - 1 + jnp.where(t > 0, 1, 0) + jnp.where(t < tiles - 1, 1, 0),
    )

    pieces = (
        (rows - plane, halo - plane),
        (rows - 2 * plane, halo - 2 * plane),
        (0, halo + rows),
        (plane, halo + rows + plane),
    )

    def halo_copy(n, kv):
        src, dst = pieces[n]
        return pltpu.make_async_remote_copy(
            src_ref=(k_hbm, v_hbm)[kv].at[pl.ds(src, plane)],
            dst_ref=(ke, ve)[kv].at[pl.ds(dst, plane)],
            send_sem=h_send.at[2 * n + kv],
            recv_sem=h_recv.at[2 * n + kv],
            device_id={"tile": t + 1 if n < 2 else t - 1},
            device_id_type=MESH,
        )

    for far in range(2):
        for kv in range(2):

            @pl.when(t < tiles - 1)
            def _():
                halo_copy(far, kv).start()

            @pl.when(t > 0)
            def _():
                halo_copy(2 + far, kv).start()

    @pl.when(t == 0)
    def _():
        ke[0:halo] = jnp.zeros((halo, model), bf16)
        ve[0:halo] = jnp.zeros((halo, model), bf16)

    @pl.when(t == tiles - 1)
    def _():
        ke[halo + rows :] = jnp.zeros((halo, model), bf16)
        ve[halo + rows :] = jnp.zeros((halo, model), bf16)

    def halo_wait(n):
        present = t > 0 if n < 2 else t < tiles - 1

        @pl.when(present)
        def _():
            for kv in range(2):
                halo_copy(n, kv).wait_recv()

    block = rows // 2
    ti = lax.broadcasted_iota(jnp.int32, (rows, rows), 0)
    tj = lax.broadcasted_iota(jnp.int32, (rows, rows), 1)
    same = ti == tj
    before = (ti < tj) & ((ti < block) == (tj < block))
    route = routes_ref[...].astype(f32)
    cols = [
        jnp.sum(jnp.where(same, route[k : k + 1], 0.0), axis=1, keepdims=True) for k in range(2)
    ]
    half = jnp.where(lax.broadcasted_iota(jnp.int32, (1, rows), 1) < block, 0.0, CAP // 2)
    for k in range(2):
        r = route[k : k + 1]
        hits = jnp.where(cols[0] == r, 1.0, 0.0) + jnp.where(cols[1] == r, 1.0, 0.0)
        rank = jnp.sum(jnp.where(before, hits, 0.0), axis=0, keepdims=True)
        column = jnp.floor(r * (1.0 / ZN))
        meta_own[k : k + 1, :] = (r - ZN * column) * (JN * CAP) + column * CAP + half + rank
    meta_own[2:4, :] = gates_ref[...]
    meta_own[4:8, :] = jnp.zeros((4, rows), f32)

    def send_meta(d):
        return pltpu.make_async_remote_copy(
            src_ref=meta_own,
            dst_ref=meta_all.at[z],
            send_sem=meta_send.at[d - 1],
            recv_sem=meta_recv.at[z],
            device_id={"tile": z_peer(d)},
            device_id_type=MESH,
        )

    for d in range(1, ZN):
        send_meta(d).start()
    meta_all[z] = meta_own[...]

    qi = lax.rem(lax.broadcasted_iota(jnp.int32, (4 * plane, keys), 0), plane)
    ki = lax.broadcasted_iota(jnp.int32, (4 * plane, keys), 1)
    kp = lax.rem(ki, plane)
    close = (jnp.abs(lax.div(qi, DP) - lax.div(kp, DP)) <= R_XL) & (
        jnp.abs(lax.rem(qi, DP) - lax.rem(kp, DP)) <= R_DP
    )
    near[...] = jnp.where(close, 0.0, -1e30)
    kcol = lax.div(lax.broadcasted_iota(jnp.int32, (1, keys), 1), plane)
    lane_head = lax.div(lax.broadcasted_iota(jnp.int32, (plane, 4 * HD), 1), HD)

    def attend(i):
        outside = ((t == 0) & (kcol < R_IL - i)) | (
            (t == tiles - 1) & (kcol > IL_DEV - 1 + R_IL - i)
        )
        bias = near[...] + jnp.where(outside, -1e30, 0.0)
        for g in range(HEADS // 4):
            lanes = slice(g * 4 * HD, (g + 1) * 4 * HD)
            q4 = q_in[i * plane : (i + 1) * plane, lanes].astype(f32) * (1.0 / HD**0.5)
            stacked = jnp.concatenate(
                [jnp.where(lane_head == h, q4, 0.0).astype(bf16) for h in range(4)], axis=0
            )
            window = slice(i * plane, i * plane + keys)
            scores = lax.dot_general(
                stacked,
                ke[window, lanes],
                (((1,), (1,)), ((), ())),
                preferred_element_type=f32,
            )
            scores = scores + bias
            highest = jnp.max(scores, axis=1, keepdims=True)
            weights = jnp.exp(scores - highest)
            totals = jnp.sum(weights, axis=1, keepdims=True)
            probs = (weights * (1.0 / totals)).astype(bf16)
            mixed = jnp.dot(probs, ve[window, lanes], preferred_element_type=f32)
            picked = mixed[0:plane]
            for h in range(1, 4):
                picked = jnp.where(lane_head == h, mixed[h * plane : (h + 1) * plane], picked)
            att[i * plane : (i + 1) * plane, lanes] = picked.astype(bf16)

    def finish(parts):
        take = lambda ref: jnp.concatenate([ref[lo : lo + n] for lo, n in parts], axis=0)
        sums = take(x_in).astype(f32) + jnp.dot(take(att), ow[...], preferred_element_type=f32)
        rounded = sums.astype(bf16)
        wide = rounded.astype(f32)
        mean_square = jnp.mean(wide * wide, axis=1, keepdims=True)
        normed = (wide * lax.rsqrt(mean_square + 1e-06) * gain_ref[...]).astype(bf16)
        at = 0
        for lo, n in parts:
            resid[lo : lo + n] = rounded[at : at + n]
            x_all[z, lo : lo + n] = normed[at : at + n]
            at += n

    chunks = ((plane, 2 * plane), (0, plane), (3 * plane, plane))

    def tile_copy(slot, c, to, send_sem):
        lo, n = chunks[c]
        return pltpu.make_async_remote_copy(
            src_ref=x_all.at[slot, pl.ds(lo, n)],
            dst_ref=x_all.at[slot, pl.ds(lo, n)],
            send_sem=send_sem,
            recv_sem=ag_recv.at[slot, c],
            device_id={"tile": to},
            device_id_type=MESH,
        )

    def send_own(c):
        @pl.when(z < ZN - 1)
        def _():
            tile_copy(z, c, t + 1, ag_send.at[0, c]).start()

        @pl.when(z > 0)
        def _():
            tile_copy(z, c, t - 1, ag_send.at[1, c]).start()

    for c in early:
        c.wait()
    halo_wait(0)
    attend(1)
    halo_wait(2)
    attend(2)
    for c in mid:
        c.wait()
    finish([chunks[0]])
    send_own(0)
    halo_wait(1)
    attend(0)
    halo_wait(3)
    attend(3)
    finish([chunks[1], chunks[2]])
    send_own(1)
    send_own(2)

    def arrive(distance):
        for c in range(len(chunks)):

            @pl.when(z - distance >= 0)
            def _():
                tile_copy(z - distance, c, t, ag_send.at[0, c]).wait_recv()

                @pl.when(z + 1 < ZN)
                def _():
                    tile_copy(z - distance, c, t + 1, fw_send.at[z - distance, c]).start()

            @pl.when(z + distance < ZN)
            def _():
                tile_copy(z + distance, c, t, ag_send.at[0, c]).wait_recv()

                @pl.when(z - 1 >= 0)
                def _():
                    tile_copy(z + distance, c, t - 1, fw_send.at[z + distance, c]).start()

    def dispatch_copy(it, d):
        return pltpu.make_async_remote_copy(
            src_ref=disp.at[it, plane_peer(d)],
            dst_ref=recv.at[it, j],
            send_sem=xs.at[it],
            recv_sem=xr.at[it],
            device_id={"tile": plane_peer(d) * ZN + z},
            device_id_type=MESH,
        )

    def return_copy(it, d):
        return pltpu.make_async_remote_copy(
            src_ref=eout.at[it, plane_peer(d)],
            dst_ref=ret.at[it, j],
            send_sem=ys.at[it],
            recv_sem=yr.at[it],
            device_id={"tile": plane_peer(d) * ZN + z},
            device_id_type=MESH,
        )

    def all_of(src, dst, it, send_sem, recv_sem):
        return pltpu.make_async_remote_copy(
            src_ref=src.at[it, pl.ds(0, JN - 1)],
            dst_ref=dst.at[it, pl.ds(0, JN - 1)],
            send_sem=send_sem.at[it],
            recv_sem=recv_sem.at[it],
            device_id={"tile": t},
            device_id_type=MESH,
        )

    slots = JN * CAP
    slot_of = lax.broadcasted_iota(jnp.int32, (slots, rows), 0).astype(jnp.float32)

    def stage_dispatch(it):
        s = tile_order(z, it)
        base = (z * slots).astype(jnp.float32)
        meta = meta_all[s] - base
        picks = (slot_of == meta[0:1]) | (slot_of == meta[1:2])
        table = picks.astype(jnp.float32).astype(jnp.bfloat16)
        picked = jnp.dot(table, x_all[s], preferred_element_type=jnp.float32).astype(jnp.bfloat16)
        disp[it] = picked.reshape(JN, CAP, model)

        def start(d, carry):
            dispatch_copy(it, d).start()
            return carry

        lax.fori_loop(1, JN, start, 0)
        recv[it, j] = disp[it, j]

    def stage_expert(it):
        all_of(disp, recv, it, xs, xr).wait_recv()
        zrows = recv[it].reshape(slots, model)
        gate_part = jnp.dot(zrows, wg[...], preferred_element_type=jnp.float32)
        up_part = jnp.dot(zrows, wu[...], preferred_element_type=jnp.float32)
        hidden = (gate_part / (1.0 + jnp.exp(-gate_part)) * up_part).astype(jnp.bfloat16)
        result = jnp.dot(hidden, wd[...], preferred_element_type=jnp.float32)
        eout[it] = result.astype(jnp.bfloat16).reshape(JN, CAP, model)

        def start(d, carry):
            return_copy(it, d).start()
            return carry

        lax.fori_loop(1, JN, start, 0)
        ret[it, j] = eout[it, j]

    def rs_copy(it):
        s = tile_order(z, it)
        return pltpu.make_async_remote_copy(
            src_ref=rs_out.at[it],
            dst_ref=rs_in.at[z],
            send_sem=rs_send.at[it],
            recv_sem=rs_recv.at[z],
            device_id={"tile": j * ZN + s},
            device_id_type=MESH,
        )

    def stage_combine(it):
        all_of(eout, ret, it, ys, yr).wait_recv()
        s = tile_order(z, it)
        base = (z * slots).astype(jnp.float32)
        meta = meta_all[s]
        pos = meta[0:2] - base
        weights = jnp.where(slot_of == pos[0:1], meta[2:3], 0.0) + jnp.where(
            slot_of == pos[1:2], meta[3:4], 0.0
        )
        part = lax.dot_general(
            weights.astype(jnp.bfloat16),
            ret[it].reshape(slots, model),
            (((0,), (0,)), ((), ())),
            preferred_element_type=jnp.float32,
        )

        @pl.when(it == 0)
        def _():
            own[...] = part

        @pl.when(it > 0)
        def _():
            rs_out[it] = part.astype(jnp.bfloat16)
            rs_copy(it).start()

    for d in range(1, ZN):
        src = lax.rem(z + d, ZN)
        pltpu.make_async_remote_copy(
            src_ref=meta_own,
            dst_ref=meta_all.at[src],
            send_sem=meta_send.at[0],
            recv_sem=meta_recv.at[src],
            device_id={"tile": t},
            device_id_type=MESH,
        ).wait_recv()
    for c in late:
        c.wait()

    def each(stage):
        def body(n, carry):
            stage(n)
            return carry

        return body

    def step(it, carry):
        for distance in range(1, ZN):

            @pl.when(it == distance)
            def _():
                arrive(distance)

        @pl.when(it < ZN)
        def _():
            stage_dispatch(it)

        lax.fori_loop(
            jnp.where(it == 2, 0, it - 1), jnp.where(it < 2, it - 1, it), each(stage_combine), 0
        )
        lax.fori_loop(
            jnp.where(it == 1, 0, it),
            jnp.where((it > 0) & (it < ZN), it + 1, it),
            each(stage_expert),
            0,
        )
        return carry

    lax.fori_loop(0, ZN + 1, step, 0)

    total = own[...] + resid[...].astype(jnp.float32)
    for d in range(1, ZN):
        src = lax.rem(z + d, ZN)
        pltpu.make_async_remote_copy(
            src_ref=rs_out.at[0],
            dst_ref=rs_in.at[src],
            send_sem=rs_send.at[0],
            recv_sem=rs_recv.at[src],
            device_id={"tile": t},
            device_id_type=MESH,
        ).wait_recv()
        total = total + rs_in[src].astype(jnp.float32)
    out_ref[...] = total.astype(jnp.bfloat16)

    for d in range(1, ZN):
        send_meta(d).wait_send()

    for n in range(4):

        @pl.when(t < tiles - 1 if n < 2 else t > 0)
        def _():
            for kv in range(2):
                halo_copy(n, kv).wait_send()

    for c in range(len(chunks)):

        @pl.when(z < ZN - 1)
        def _():
            tile_copy(z, c, t, ag_send.at[0, c]).wait_send()

        @pl.when(z > 0)
        def _():
            tile_copy(z, c, t, ag_send.at[1, c]).wait_send()

        for distance in range(1, ZN):

            @pl.when((z - distance >= 0) & (z + 1 < ZN))
            def _():
                tile_copy(z - distance, c, t, fw_send.at[z - distance, c]).wait_send()

            @pl.when((z + distance < ZN) & (z - 1 >= 0))
            def _():
                tile_copy(z + distance, c, t, fw_send.at[z + distance, c]).wait_send()

    def drain(it, carry):
        all_of(disp, recv, it, xs, xr).wait_send()
        all_of(eout, ret, it, ys, yr).wait_send()

        @pl.when(it > 0)
        def _():
            rs_copy(it).wait_send()

        return carry

    lax.fori_loop(0, ZN, drain, 0)


def local(
    inputs,
    queries,
    key_vectors,
    values,
    out_weight,
    norm_gain,
    routes,
    route_gates,
    w_gate,
    w_up,
    w_down,
):
    rows, model = inputs.shape
    wide = w_gate.shape[2]
    plane = XL * DP
    halo = R_IL * plane
    bf16 = jnp.bfloat16
    f32 = jnp.float32
    vmem = pl.BlockSpec(memory_space=pltpu.VMEM)
    anywhere = pl.BlockSpec(memory_space=pl.ANY)
    dma = pltpu.SemaphoreType.DMA
    return pl.pallas_call(
        layer_kernel,
        out_shape=jax.ShapeDtypeStruct((rows, model), bf16),
        in_specs=[anywhere] * 5 + [vmem] * 3 + [anywhere] * 3,
        out_specs=vmem,
        scratch_shapes=[
            pltpu.VMEM((rows, model), bf16),
            pltpu.VMEM((rows, model), bf16),
            pltpu.VMEM((rows + 2 * halo, model), bf16),
            pltpu.VMEM((rows + 2 * halo, model), bf16),
            pltpu.VMEM((model, model), bf16),
            pltpu.VMEM((rows, model), bf16),
            pltpu.VMEM((4 * plane, (2 * R_IL + 1) * plane), f32),
            pltpu.VMEM((model, wide), bf16),
            pltpu.VMEM((model, wide), bf16),
            pltpu.VMEM((wide, model), bf16),
            pltpu.VMEM((8, rows), f32),
            pltpu.VMEM((ZN, 8, rows), f32),
            pltpu.VMEM((ZN, rows, model), bf16),
            pltpu.VMEM((rows, model), bf16),
            pltpu.VMEM((ZN, JN, CAP, model), bf16),
            pltpu.VMEM((ZN, JN, CAP, model), bf16),
            pltpu.VMEM((ZN, JN, CAP, model), bf16),
            pltpu.VMEM((ZN, JN, CAP, model), bf16),
            pltpu.VMEM((rows, model), f32),
            pltpu.VMEM((ZN, rows, model), bf16),
            pltpu.VMEM((ZN, rows, model), bf16),
            dma((8,)),
            dma((8,)),
            dma((8,)),
            dma((3,)),
            dma((ZN,)),
            dma((2, 3)),
            dma((ZN, 3)),
            dma((ZN, 3)),
            dma((ZN,)),
            dma((ZN,)),
            dma((ZN,)),
            dma((ZN,)),
            dma((ZN,)),
            dma((ZN,)),
        ],
        compiler_params=pltpu.CompilerParams(
            collective_id=1, has_side_effects=True, vmem_limit_bytes=58 * 1024 * 1024
        ),
    )(
        inputs,
        queries,
        key_vectors,
        values,
        out_weight,
        norm_gain.reshape(1, model),
        routes.T,
        route_gates.T,
        w_gate,
        w_up,
        w_down,
    )


def solution(mesh):
    return jax.shard_map(
        local,
        mesh=mesh,
        in_specs=(
            P(("rep", "tile"), None),
            P(("rep", "tile"), None),
            P(("rep", "tile"), None),
            P(("rep", "tile"), None),
            P(),
            P(),
            P(("rep", "tile"), None),
            P(("rep", "tile"), None),
            P("tile", None, None),
            P("tile", None, None),
            P("tile", None, None),
        ),
        out_specs=P(("rep", "tile"), None),
        check_vma=False,
    )
```

```python
import jax
import jax.numpy as jnp
from jax import lax
from jax.experimental import pallas as pl
from jax.experimental.pallas import tpu as pltpu
from jax.sharding import PartitionSpec as P

HEADS = 16
HD = 64
IL_DEV = 4
XL = 8
DP = 8
R_IL = 2
R_XL = 2
R_DP = 2
ZN = 4
JN = 16
CAP = 8
PIECES = 2 * ZN
MESH = pl.DeviceIdType.MESH


def tile_order(z, it):
    low = jnp.where(z == 0, it, lax.rem(it + 1, ZN))
    mirrored = jnp.where(z == 3, it, lax.rem(it + 1, ZN))
    return jnp.where(z < 2, low, 3 - mirrored)


def layer_kernel(
    x_hbm,
    q_hbm,
    k_hbm,
    v_hbm,
    ow_hbm,
    gain_ref,
    routes_ref,
    gates_ref,
    wg_hbm,
    wu_hbm,
    wd_hbm,
    out_ref,
    x_in,
    q_in,
    ke,
    ve,
    ow,
    att,
    near,
    wg,
    wu,
    wd,
    meta_own,
    meta_all,
    x_all,
    resid,
    disp,
    recv,
    eout,
    ret,
    own,
    partial,
    rs_out,
    merge_in,
    final_in,
    l_sem,
    h_send,
    h_recv,
    meta_send,
    meta_recv,
    ag_send,
    fw_send,
    ag_recv,
    xs,
    xr,
    ys,
    yr,
    rs_send,
    merge_recv,
    final_recv,
):
    t = lax.axis_index("tile")
    tiles = lax.axis_size("tile")
    z = lax.rem(t, ZN)
    j = lax.div(t, ZN)
    rows = x_in.shape[0]
    model = x_in.shape[1]
    plane = XL * DP
    halo = R_IL * plane
    keys = (2 * R_IL + 1) * plane
    bf16 = jnp.bfloat16
    f32 = jnp.float32

    def local_copy(src, dst, n):
        return pltpu.make_async_copy(src, dst, l_sem.at[n])

    early = [
        local_copy(k_hbm, ke.at[pl.ds(halo, rows)], 0),
        local_copy(v_hbm, ve.at[pl.ds(halo, rows)], 1),
        local_copy(q_hbm, q_in, 2),
    ]
    mid = [local_copy(x_hbm, x_in, 3), local_copy(ow_hbm, ow, 4)]
    late = [
        local_copy(wg_hbm.at[0], wg, 5),
        local_copy(wu_hbm.at[0], wu, 6),
        local_copy(wd_hbm.at[0], wd, 7),
    ]

    barrier = pltpu.get_barrier_semaphore()

    def greet(tile):
        pl.semaphore_signal(barrier, inc=1, device_id={"tile": tile}, device_id_type=MESH)

    def z_peer(d):
        return j * ZN + lax.rem(z + d, ZN)

    def plane_peer(d):
        return lax.rem(j + d, JN)

    @pl.when(t > 0)
    def _():
        greet(t - 1)

    @pl.when(t < tiles - 1)
    def _():
        greet(t + 1)

    for d in range(1, ZN):
        greet(z_peer(d))

    def greet_plane(d, carry):
        greet(plane_peer(d) * ZN + z)
        return carry

    lax.fori_loop(1, JN, greet_plane, 0)
    for c in early + mid + late:
        c.start()
    pl.semaphore_wait(
        barrier,
        JN - 1 + ZN - 1 + jnp.where(t > 0, 1, 0) + jnp.where(t < tiles - 1, 1, 0),
    )

    def halo_copy(n, kv):
        src, dst = ((rows - halo, 0), (0, halo + rows))[n]
        return pltpu.make_async_remote_copy(
            src_ref=(k_hbm, v_hbm)[kv].at[pl.ds(src, halo)],
            dst_ref=(ke, ve)[kv].at[pl.ds(dst, halo)],
            send_sem=h_send.at[2 * n + kv],
            recv_sem=h_recv.at[2 * n + kv],
            device_id={"tile": t + 1 if n == 0 else t - 1},
            device_id_type=MESH,
        )

    @pl.when(t < tiles - 1)
    def _():
        for kv in range(2):
            halo_copy(0, kv).start()

    @pl.when(t == 0)
    def _():
        ke[0:halo] = jnp.zeros((halo, model), bf16)
        ve[0:halo] = jnp.zeros((halo, model), bf16)

    @pl.when(t == tiles - 1)
    def _():
        ke[halo + rows :] = jnp.zeros((halo, model), bf16)
        ve[halo + rows :] = jnp.zeros((halo, model), bf16)

    def halo_wait(n):
        @pl.when(t > 0 if n == 0 else t < tiles - 1)
        def _():
            for kv in range(2):
                halo_copy(n, kv).wait_recv()

    block = rows // 2
    ti = lax.broadcasted_iota(jnp.int32, (rows, rows), 0)
    tj = lax.broadcasted_iota(jnp.int32, (rows, rows), 1)
    same = ti == tj
    before = (ti < tj) & ((ti < block) == (tj < block))
    route = routes_ref[...].astype(f32)
    cols = [
        jnp.sum(jnp.where(same, route[k : k + 1], 0.0), axis=1, keepdims=True) for k in range(2)
    ]
    for k in range(2):
        r = route[k : k + 1]
        hits = jnp.where(cols[0] == r, 1.0, 0.0) + jnp.where(cols[1] == r, 1.0, 0.0)
        rank = jnp.sum(jnp.where(before, hits, 0.0), axis=0, keepdims=True)
        column = jnp.floor(r * (1.0 / ZN))
        meta_own[k : k + 1, :] = (r - ZN * column) * (JN * CAP) + column * CAP + rank
    meta_own[2:4, :] = gates_ref[...]
    meta_own[4:8, :] = jnp.zeros((4, rows), f32)

    def send_meta(d):
        return pltpu.make_async_remote_copy(
            src_ref=meta_own,
            dst_ref=meta_all.at[z],
            send_sem=meta_send.at[d - 1],
            recv_sem=meta_recv.at[z],
            device_id={"tile": z_peer(d)},
            device_id_type=MESH,
        )

    for d in range(1, ZN):
        send_meta(d).start()
    meta_all[z] = meta_own[...]

    @pl.when(t < tiles - 1)
    def _():
        for kv in range(2):
            halo_copy(0, kv).wait_send()

    @pl.when(t > 0)
    def _():
        for kv in range(2):
            halo_copy(1, kv).start()

    qi = lax.rem(lax.broadcasted_iota(jnp.int32, (4 * plane, keys), 0), plane)
    ki = lax.broadcasted_iota(jnp.int32, (4 * plane, keys), 1)
    kp = lax.rem(ki, plane)
    close = (jnp.abs(lax.div(qi, DP) - lax.div(kp, DP)) <= R_XL) & (
        jnp.abs(lax.rem(qi, DP) - lax.rem(kp, DP)) <= R_DP
    )
    near[...] = jnp.where(close, 0.0, -1e30)
    kcol = lax.div(lax.broadcasted_iota(jnp.int32, (1, keys), 1), plane)
    lane_head = lax.div(lax.broadcasted_iota(jnp.int32, (plane, 4 * HD), 1), HD)

    def attend(i):
        outside = ((t == 0) & (kcol < R_IL - i)) | (
            (t == tiles - 1) & (kcol > IL_DEV - 1 + R_IL - i)
        )
        bias = near[...] + jnp.where(outside, -1e30, 0.0)
        for g in range(HEADS // 4):
            lanes = slice(g * 4 * HD, (g + 1) * 4 * HD)
            q4 = q_in[i * plane : (i + 1) * plane, lanes].astype(f32) * (1.0 / HD**0.5)
            stacked = jnp.concatenate(
                [jnp.where(lane_head == h, q4, 0.0).astype(bf16) for h in range(4)], axis=0
            )
            window = slice(i * plane, i * plane + keys)
            scores = lax.dot_general(
                stacked,
                ke[window, lanes],
                (((1,), (1,)), ((), ())),
                preferred_element_type=f32,
            )
            scores = scores + bias
            highest = jnp.max(scores, axis=1, keepdims=True)
            weights = jnp.exp(scores - highest)
            totals = jnp.sum(weights, axis=1, keepdims=True)
            probs = (weights * (1.0 / totals)).astype(bf16)
            mixed = jnp.dot(probs, ve[window, lanes], preferred_element_type=f32)
            picked = mixed[0:plane]
            for h in range(1, 4):
                picked = jnp.where(lane_head == h, mixed[h * plane : (h + 1) * plane], picked)
            att[i * plane : (i + 1) * plane, lanes] = picked.astype(bf16)

    def finish(h):
        part = slice(h * block, (h + 1) * block)
        sums = x_in[part].astype(f32) + jnp.dot(att[part], ow[...], preferred_element_type=f32)
        rounded = sums.astype(bf16)
        wide = rounded.astype(f32)
        mean_square = jnp.mean(wide * wide, axis=1, keepdims=True)
        resid[part] = rounded
        x_all[z, part] = (wide * lax.rsqrt(mean_square + 1e-06) * gain_ref[...]).astype(bf16)

    def tile_copy(slot, h, to, send_sem):
        part = pl.ds(pl.multiple_of(h * block, block), block)
        return pltpu.make_async_remote_copy(
            src_ref=x_all.at[slot, part],
            dst_ref=x_all.at[slot, part],
            send_sem=send_sem,
            recv_sem=ag_recv.at[slot, h],
            device_id={"tile": to},
            device_id_type=MESH,
        )

    def send_own(c):
        @pl.when(z < ZN - 1)
        def _():
            tile_copy(z, c, t + 1, ag_send.at[0, c]).start()

        @pl.when(z > 0)
        def _():
            tile_copy(z, c, t - 1, ag_send.at[1, c]).start()

    def arrive(distance, h):
        @pl.when(z - distance >= 0)
        def _():
            tile_copy(z - distance, h, t, ag_send.at[0, h]).wait_recv()

            @pl.when(z + 1 < ZN)
            def _():
                tile_copy(z - distance, h, t + 1, fw_send.at[z - distance, h]).start()

        @pl.when(z + distance < ZN)
        def _():
            tile_copy(z + distance, h, t, ag_send.at[0, h]).wait_recv()

            @pl.when(z - 1 >= 0)
            def _():
                tile_copy(z + distance, h, t - 1, fw_send.at[z + distance, h]).start()

    def dispatch_copy(m, d):
        return pltpu.make_async_remote_copy(
            src_ref=disp.at[m, plane_peer(d)],
            dst_ref=recv.at[m, j],
            send_sem=xs.at[m],
            recv_sem=xr.at[m],
            device_id={"tile": plane_peer(d) * ZN + z},
            device_id_type=MESH,
        )

    def return_copy(m, d):
        return pltpu.make_async_remote_copy(
            src_ref=eout.at[m, plane_peer(d)],
            dst_ref=ret.at[m, j],
            send_sem=ys.at[m],
            recv_sem=yr.at[m],
            device_id={"tile": plane_peer(d) * ZN + z},
            device_id_type=MESH,
        )

    def all_of(src, dst, m, send_sem, recv_sem):
        return pltpu.make_async_remote_copy(
            src_ref=src.at[m, pl.ds(0, JN - 1)],
            dst_ref=dst.at[m, pl.ds(0, JN - 1)],
            send_sem=send_sem.at[m],
            recv_sem=recv_sem.at[m],
            device_id={"tile": t},
            device_id_type=MESH,
        )

    slots = JN * CAP
    slot_of = lax.broadcasted_iota(jnp.int32, (slots, block), 0).astype(f32)
    end = (z == 0) | (z == ZN - 1)
    inward = jnp.where(z < 2, 1, -1)

    def piece_meta(m):
        h = lax.rem(m, 2)
        meta = meta_all[tile_order(z, lax.div(m, 2))]
        meta = jnp.where(h == 0, meta[:, 0:block], meta[:, block:])
        return meta[0:2] - (z * slots).astype(f32), meta[2:4]

    def stage_dispatch(m):
        s = tile_order(z, lax.div(m, 2))
        pos, _ = piece_meta(m)
        table = jnp.where((slot_of == pos[0:1]) | (slot_of == pos[1:2]), 1.0, 0.0).astype(bf16)
        part = pl.ds(pl.multiple_of(lax.rem(m, 2) * block, block), block)
        picked = jnp.dot(table, x_all[s, part], preferred_element_type=f32)
        disp[m] = picked.reshape(JN, CAP, model).astype(bf16)

        def start(d, carry):
            dispatch_copy(m, d).start()
            return carry

        lax.fori_loop(1, JN, start, 0)
        recv[m, j] = disp[m, j]

    def stage_expert(m):
        all_of(disp, recv, m, xs, xr).wait_recv()
        zrows = recv[m].astype(f32).reshape(slots, model).astype(bf16)
        gate_part = jnp.dot(zrows, wg[...], preferred_element_type=f32)
        up_part = jnp.dot(zrows, wu[...], preferred_element_type=f32)
        hidden = (gate_part / (1.0 + jnp.exp(-gate_part)) * up_part).astype(bf16)
        result = jnp.dot(hidden, wd[...], preferred_element_type=f32)
        eout[m] = result.reshape(JN, CAP, model).astype(bf16)

        def start(d, carry):
            return_copy(m, d).start()
            return carry

        lax.fori_loop(1, JN, start, 0)
        ret[m, j] = eout[m, j]

    def sum_copy(m, dst, recv_sem, to):
        return pltpu.make_async_remote_copy(
            src_ref=rs_out.at[m],
            dst_ref=dst,
            send_sem=rs_send.at[m],
            recv_sem=recv_sem,
            device_id={"tile": to},
            device_id_type=MESH,
        )

    def to_merge(m, h):
        kind = jnp.where(end, 0, 1)
        return sum_copy(m, merge_in.at[kind, h], merge_recv.at[kind, h], t + inward)

    def to_final(m, h, side):
        s = tile_order(z, lax.div(m, 2))
        return sum_copy(m, final_in.at[side, h], final_recv.at[side, h], j * ZN + s)

    def next_side(m):
        return jnp.where(z < tile_order(z, lax.div(m, 2)), 0, 1)

    def stage_combine(m):
        all_of(eout, ret, m, ys, yr).wait_recv()
        it = lax.div(m, 2)
        h = lax.rem(m, 2)
        pos, gate = piece_meta(m)
        weights = jnp.where(slot_of == pos[0:1], gate[0:1], 0.0) + jnp.where(
            slot_of == pos[1:2], gate[1:2], 0.0
        )
        part = lax.dot_general(
            weights.astype(bf16),
            ret[m].astype(f32).reshape(slots, model).astype(bf16),
            (((0,), (0,)), ((), ())),
            preferred_element_type=f32,
        )

        @pl.when(it == 0)
        def _():
            own[pl.ds(pl.multiple_of(h * block, block), block)] = part

        @pl.when((it == 1) & end)
        def _():
            rs_out[m] = part.astype(bf16)
            to_final(m, h, next_side(m)).start()

        @pl.when((it == 1) & ~end)
        def _():
            partial[h] = part

        @pl.when(it == 2)
        def _():
            rs_out[m] = part.astype(bf16)
            to_merge(m, h).start()

        @pl.when((it == 3) & end)
        def _():
            rs_out[m] = part.astype(bf16)
            to_final(m, h, 2).start()

        @pl.when((it == 3) & ~end)
        def _():
            sum_copy(m, merge_in.at[1, h], merge_recv.at[1, h], t).wait_recv()
            rs_out[m] = (part + merge_in[1, h].astype(f32)).astype(bf16)
            to_final(m, h, next_side(m)).start()

    def stage_merge(m):
        h = lax.rem(m, 2)

        @pl.when(~end)
        def _():
            sum_copy(m, merge_in.at[0, h], merge_recv.at[0, h], t).wait_recv()
            rs_out[m] = (partial[h] + merge_in[0, h].astype(f32)).astype(bf16)
            to_final(m, h, next_side(m)).start()

    for c in early:
        c.wait()
    halo_wait(0)
    attend(0)
    attend(1)
    for c in mid:
        c.wait()
    finish(0)
    send_own(0)
    for d in range(1, ZN):
        src = lax.rem(z + d, ZN)
        pltpu.make_async_remote_copy(
            src_ref=meta_own,
            dst_ref=meta_all.at[src],
            send_sem=meta_send.at[0],
            recv_sem=meta_recv.at[src],
            device_id={"tile": t},
            device_id_type=MESH,
        ).wait_recv()
    for c in late:
        c.wait()
    halo_wait(1)
    attend(2)
    attend(3)
    finish(1)
    send_own(1)

    def step(k, carry):
        for distance in range(1, ZN):

            @pl.when(lax.div(k, 2) == distance)
            def _():
                arrive(distance, lax.rem(k, 2))

        @pl.when(k < PIECES)
        def _():
            stage_dispatch(k)

        @pl.when((k >= 1) & (k < PIECES + 1))
        def _():
            stage_expert(k - 1)

        @pl.when(k >= 2)
        def _():
            stage_combine(k - 2)

        @pl.when((k == 7) | (k == 8))
        def _():
            stage_merge(k - 5)

        return carry

    lax.fori_loop(0, PIECES + 2, step, 0)

    def add_final(side, h):
        sum_copy(0, final_in.at[side, h], final_recv.at[side, h], t).wait_recv()
        part = slice(h * block, (h + 1) * block)
        own[part] = own[part] + final_in[side, h].astype(f32)

    for h in range(2):

        @pl.when(z > 0)
        def _():
            add_final(0, h)

        @pl.when(z < ZN - 1)
        def _():
            add_final(1, h)

        @pl.when(end)
        def _():
            add_final(2, h)

        part = slice(h * block, (h + 1) * block)
        out_ref[part] = (own[part] + resid[part].astype(f32)).astype(bf16)

    for d in range(1, ZN):
        send_meta(d).wait_send()

    @pl.when(t > 0)
    def _():
        for kv in range(2):
            halo_copy(1, kv).wait_send()

    for h in range(2):

        @pl.when(z < ZN - 1)
        def _():
            tile_copy(z, h, t, ag_send.at[0, h]).wait_send()

        @pl.when(z > 0)
        def _():
            tile_copy(z, h, t, ag_send.at[1, h]).wait_send()

        for distance in range(1, ZN):

            @pl.when((z - distance >= 0) & (z + 1 < ZN))
            def _():
                tile_copy(z - distance, h, t, fw_send.at[z - distance, h]).wait_send()

            @pl.when((z + distance < ZN) & (z - 1 >= 0))
            def _():
                tile_copy(z + distance, h, t, fw_send.at[z + distance, h]).wait_send()

    def drain(m, carry):
        all_of(disp, recv, m, xs, xr).wait_send()
        all_of(eout, ret, m, ys, yr).wait_send()

        @pl.when(m >= 2)
        def _():
            sum_copy(m, final_in.at[0, 0], final_recv.at[0, 0], t).wait_send()

        return carry

    lax.fori_loop(0, PIECES, drain, 0)


def local(
    inputs,
    queries,
    key_vectors,
    values,
    out_weight,
    norm_gain,
    routes,
    route_gates,
    w_gate,
    w_up,
    w_down,
):
    rows, model = inputs.shape
    wide = w_gate.shape[2]
    plane = XL * DP
    halo = R_IL * plane
    bf16 = jnp.bfloat16
    f32 = jnp.float32
    vmem = pl.BlockSpec(memory_space=pltpu.VMEM)
    anywhere = pl.BlockSpec(memory_space=pl.ANY)
    dma = pltpu.SemaphoreType.DMA
    return pl.pallas_call(
        layer_kernel,
        out_shape=jax.ShapeDtypeStruct((rows, model), bf16),
        in_specs=[anywhere] * 5 + [vmem] * 3 + [anywhere] * 3,
        out_specs=vmem,
        scratch_shapes=[
            pltpu.VMEM((rows, model), bf16),
            pltpu.VMEM((rows, model), bf16),
            pltpu.VMEM((rows + 2 * halo, model), bf16),
            pltpu.VMEM((rows + 2 * halo, model), bf16),
            pltpu.VMEM((model, model), bf16),
            pltpu.VMEM((rows, model), bf16),
            pltpu.VMEM((4 * plane, (2 * R_IL + 1) * plane), f32),
            pltpu.VMEM((model, wide), bf16),
            pltpu.VMEM((model, wide), bf16),
            pltpu.VMEM((wide, model), bf16),
            pltpu.VMEM((8, rows), f32),
            pltpu.VMEM((ZN, 8, rows), f32),
            pltpu.VMEM((ZN, rows, model), bf16),
            pltpu.VMEM((rows, model), bf16),
            pltpu.VMEM((PIECES, JN, CAP, model), bf16),
            pltpu.VMEM((PIECES, JN, CAP, model), bf16),
            pltpu.VMEM((PIECES, JN, CAP, model), bf16),
            pltpu.VMEM((PIECES, JN, CAP, model), bf16),
            pltpu.VMEM((rows, model), f32),
            pltpu.VMEM((2, rows // 2, model), f32),
            pltpu.VMEM((PIECES, rows // 2, model), bf16),
            pltpu.VMEM((2, 2, rows // 2, model), bf16),
            pltpu.VMEM((3, 2, rows // 2, model), bf16),
            dma((8,)),
            dma((4,)),
            dma((4,)),
            dma((3,)),
            dma((ZN,)),
            dma((2, 2)),
            dma((ZN, 2)),
            dma((ZN, 2)),
            dma((PIECES,)),
            dma((PIECES,)),
            dma((PIECES,)),
            dma((PIECES,)),
            dma((PIECES,)),
            dma((2, 2)),
            dma((3, 2)),
        ],
        compiler_params=pltpu.CompilerParams(
            collective_id=1, has_side_effects=True, vmem_limit_bytes=58 * 1024 * 1024
        ),
    )(
        inputs,
        queries,
        key_vectors,
        values,
        out_weight,
        norm_gain.reshape(1, model),
        routes.T,
        route_gates.T,
        w_gate,
        w_up,
        w_down,
    )


def solution(mesh):
    return jax.shard_map(
        local,
        mesh=mesh,
        in_specs=(
            P(("rep", "tile"), None),
            P(("rep", "tile"), None),
            P(("rep", "tile"), None),
            P(("rep", "tile"), None),
            P(),
            P(),
            P(("rep", "tile"), None),
            P(("rep", "tile"), None),
            P("tile", None, None),
            P("tile", None, None),
            P("tile", None, None),
        ),
        out_specs=P(("rep", "tile"), None),
        check_vma=False,
    )
```

```python
import jax
import jax.numpy as jnp
from jax import lax
from jax.experimental import pallas as pl
from jax.experimental.pallas import tpu as pltpu
from jax.sharding import PartitionSpec as P

HEADS = 16
HD = 64
IL_DEV = 4
XL = 8
DP = 8
R_IL = 2
R_XL = 2
R_DP = 2
ZN = 4
JN = 16
CAP = 8
PIECES = 2 * ZN
MESH = pl.DeviceIdType.MESH


def layer_kernel(
    x_hbm,
    q_hbm,
    k_hbm,
    v_hbm,
    ow_hbm,
    gain_ref,
    routes_ref,
    gates_ref,
    wg_hbm,
    wu_hbm,
    wd_hbm,
    out_ref,
    x_in,
    q_in,
    ke,
    ve,
    ow,
    att,
    near,
    wg,
    wu,
    wd,
    meta_own,
    meta_all,
    x_all,
    resid,
    disp,
    recv,
    eout,
    ret,
    own,
    partial,
    rs_out,
    merge_in,
    final_in,
    l_sem,
    h_send,
    h_recv,
    meta_send,
    meta_recv,
    ag_send,
    fw_send,
    ag_recv,
    xs,
    xr,
    ys,
    yr,
    rs_send,
    merge_recv,
    final_recv,
):
    t = lax.axis_index("tile")
    tiles = lax.axis_size("tile")
    z = lax.rem(t, ZN)
    j = lax.div(t, ZN)
    rows = x_in.shape[0]
    model = x_in.shape[1]
    plane = XL * DP
    halo = R_IL * plane
    keys = (2 * R_IL + 1) * plane
    bf16 = jnp.bfloat16
    f32 = jnp.float32

    def local_copy(src, dst, n):
        return pltpu.make_async_copy(src, dst, l_sem.at[n])

    early = [
        local_copy(k_hbm, ke.at[pl.ds(halo, rows)], 0),
        local_copy(v_hbm, ve.at[pl.ds(halo, rows)], 1),
        local_copy(q_hbm, q_in, 2),
    ]
    mid = [local_copy(x_hbm, x_in, 3), local_copy(ow_hbm, ow, 4)]
    late = [
        local_copy(wg_hbm.at[0], wg, 5),
        local_copy(wu_hbm.at[0], wu, 6),
        local_copy(wd_hbm.at[0], wd, 7),
    ]

    barrier = pltpu.get_barrier_semaphore()

    def greet(tile):
        pl.semaphore_signal(barrier, inc=1, device_id={"tile": tile}, device_id_type=MESH)

    def z_peer(d):
        return j * ZN + lax.rem(z + d, ZN)

    def plane_peer(d):
        return lax.rem(j + d, JN)

    @pl.when(t > 0)
    def _():
        greet(t - 1)

    @pl.when(t < tiles - 1)
    def _():
        greet(t + 1)

    for d in range(1, ZN):
        greet(z_peer(d))

    def greet_plane(d, carry):
        greet(plane_peer(d) * ZN + z)
        return carry

    lax.fori_loop(1, JN, greet_plane, 0)
    for c in early + mid + late:
        c.start()
    pl.semaphore_wait(
        barrier,
        JN - 1 + ZN - 1 + jnp.where(t > 0, 1, 0) + jnp.where(t < tiles - 1, 1, 0),
    )

    def halo_copy(n, kv):
        src, dst = ((rows - halo, 0), (0, halo + rows))[n]
        return pltpu.make_async_remote_copy(
            src_ref=(k_hbm, v_hbm)[kv].at[pl.ds(src, halo)],
            dst_ref=(ke, ve)[kv].at[pl.ds(dst, halo)],
            send_sem=h_send.at[2 * n + kv],
            recv_sem=h_recv.at[2 * n + kv],
            device_id={"tile": t + 1 if n == 0 else t - 1},
            device_id_type=MESH,
        )

    @pl.when(t < tiles - 1)
    def _():
        for kv in range(2):
            halo_copy(0, kv).start()

    @pl.when(t == 0)
    def _():
        ke[0:halo] = jnp.zeros((halo, model), bf16)
        ve[0:halo] = jnp.zeros((halo, model), bf16)

    @pl.when(t == tiles - 1)
    def _():
        ke[halo + rows :] = jnp.zeros((halo, model), bf16)
        ve[halo + rows :] = jnp.zeros((halo, model), bf16)

    def halo_wait(n):
        @pl.when(t > 0 if n == 0 else t < tiles - 1)
        def _():
            for kv in range(2):
                halo_copy(n, kv).wait_recv()

    block = rows // 2
    ti = lax.broadcasted_iota(jnp.int32, (rows, rows), 0)
    tj = lax.broadcasted_iota(jnp.int32, (rows, rows), 1)
    same = ti == tj
    before = (ti < tj) & ((ti < block) == (tj < block))
    route = routes_ref[...].astype(f32)
    cols = [
        jnp.sum(jnp.where(same, route[k : k + 1], 0.0), axis=1, keepdims=True) for k in range(2)
    ]
    for k in range(2):
        r = route[k : k + 1]
        hits = jnp.where(cols[0] == r, 1.0, 0.0) + jnp.where(cols[1] == r, 1.0, 0.0)
        rank = jnp.sum(jnp.where(before, hits, 0.0), axis=0, keepdims=True)
        column = jnp.floor(r * (1.0 / ZN))
        meta_own[k : k + 1, :] = (r - ZN * column) * (JN * CAP) + column * CAP + rank
    meta_own[2:4, :] = gates_ref[...]
    meta_own[4:8, :] = jnp.zeros((4, rows), f32)

    def send_meta(d):
        return pltpu.make_async_remote_copy(
            src_ref=meta_own,
            dst_ref=meta_all.at[z],
            send_sem=meta_send.at[d - 1],
            recv_sem=meta_recv.at[z],
            device_id={"tile": z_peer(d)},
            device_id_type=MESH,
        )

    for d in range(1, ZN):
        send_meta(d).start()
    meta_all[z] = meta_own[...]

    for kv in range(2):

        @pl.when(t < tiles - 1)
        def _():
            halo_copy(0, kv).wait_send()

        @pl.when(t > 0)
        def _():
            halo_copy(1, kv).start()

    qi = lax.rem(lax.broadcasted_iota(jnp.int32, (4 * plane, keys), 0), plane)
    ki = lax.broadcasted_iota(jnp.int32, (4 * plane, keys), 1)
    kp = lax.rem(ki, plane)
    close = (jnp.abs(lax.div(qi, DP) - lax.div(kp, DP)) <= R_XL) & (
        jnp.abs(lax.rem(qi, DP) - lax.rem(kp, DP)) <= R_DP
    )
    near[...] = jnp.where(close, 0.0, -1e30)
    kcol = lax.div(lax.broadcasted_iota(jnp.int32, (1, keys), 1), plane)
    lane_head = lax.div(lax.broadcasted_iota(jnp.int32, (plane, 4 * HD), 1), HD)

    def attend(i):
        outside = ((t == 0) & (kcol < R_IL - i)) | (
            (t == tiles - 1) & (kcol > IL_DEV - 1 + R_IL - i)
        )
        bias = near[...] + jnp.where(outside, -1e30, 0.0)
        for g in range(HEADS // 4):
            lanes = slice(g * 4 * HD, (g + 1) * 4 * HD)
            q4 = q_in[i * plane : (i + 1) * plane, lanes].astype(f32) * (1.0 / HD**0.5)
            stacked = jnp.concatenate(
                [jnp.where(lane_head == h, q4, 0.0).astype(bf16) for h in range(4)], axis=0
            )
            window = slice(i * plane, i * plane + keys)
            scores = lax.dot_general(
                stacked,
                ke[window, lanes],
                (((1,), (1,)), ((), ())),
                preferred_element_type=f32,
            )
            scores = scores + bias
            highest = jnp.max(scores, axis=1, keepdims=True)
            weights = jnp.exp(scores - highest)
            totals = jnp.sum(weights, axis=1, keepdims=True)
            probs = (weights * (1.0 / totals)).astype(bf16)
            mixed = jnp.dot(probs, ve[window, lanes], preferred_element_type=f32)
            picked = mixed[0:plane]
            for h in range(1, 4):
                picked = jnp.where(lane_head == h, mixed[h * plane : (h + 1) * plane], picked)
            att[i * plane : (i + 1) * plane, lanes] = picked.astype(bf16)

    def finish(h):
        part = slice(h * block, (h + 1) * block)
        sums = x_in[part].astype(f32) + jnp.dot(att[part], ow[...], preferred_element_type=f32)
        rounded = sums.astype(bf16)
        wide = rounded.astype(f32)
        mean_square = jnp.mean(wide * wide, axis=1, keepdims=True)
        resid[part] = rounded
        x_all[z, part] = (wide * lax.rsqrt(mean_square + 1e-06) * gain_ref[...]).astype(bf16)

    def tile_copy(slot, h, to, send_sem):
        part = pl.ds(pl.multiple_of(h * block, block), block)
        return pltpu.make_async_remote_copy(
            src_ref=x_all.at[slot, part],
            dst_ref=x_all.at[slot, part],
            send_sem=send_sem,
            recv_sem=ag_recv.at[slot, h],
            device_id={"tile": to},
            device_id_type=MESH,
        )

    end = (z == 0) | (z == ZN - 1)
    inward = jnp.where(z < 2, 1, -1)
    t_in = t + inward
    t_out = jnp.where(end, t, t - inward)
    in1 = z + inward
    in2 = z + 2 * inward
    out1 = jnp.where(end, z, z - inward)

    def own_in(h):
        return tile_copy(z, h, t_in, ag_send.at[0, h])

    def own_out(h):
        return tile_copy(z, h, t_out, ag_send.at[1, h])

    def forward(slot, h, to):
        return tile_copy(slot, h, to, fw_send.at[slot, h])

    def arrived(slot, h):
        tile_copy(slot, h, t_in, ag_send.at[0, h]).wait_recv()

    def piece(m):
        h = jnp.where((m == 1) | (m >= 5), 1, 0)
        at_end = jnp.where(m < 2, 0, jnp.where(m < 5, m - 1, 8 - m))
        at_mid = jnp.where((m == 4) | (m == 6), -1, jnp.where((m == 3) | (m == 5), 2, 1))
        at_mid = jnp.where(m < 2, 0, at_mid)
        return z + inward * jnp.where(end, at_end, at_mid), h

    def arrive(k):
        @pl.when(end & (k >= 2) & (k < PIECES))
        def _():
            slot, h = piece(k)
            arrived(slot, h)

        @pl.when(~end & (k == 2))
        def _():
            arrived(in1, 0)
            forward(in1, 0, t_out).start()
            arrived(out1, 0)
            forward(out1, 0, t_in).start()

        @pl.when(~end & (k == 3))
        def _():
            arrived(out1, 1)
            forward(out1, 1, t_in).start()
            own_in(1).start()
            arrived(in2, 0)
            forward(in2, 0, t_out).start()

        @pl.when(~end & (k == 5))
        def _():
            arrived(in2, 1)
            forward(in2, 1, t_out).start()

        @pl.when(~end & (k == 7))
        def _():
            arrived(in1, 1)
            forward(in1, 1, t_out).start()
            own_out(1).start()

    def dispatch_copy(m, d):
        return pltpu.make_async_remote_copy(
            src_ref=disp.at[m, plane_peer(d)],
            dst_ref=recv.at[m, j],
            send_sem=xs.at[m],
            recv_sem=xr.at[m],
            device_id={"tile": plane_peer(d) * ZN + z},
            device_id_type=MESH,
        )

    def return_copy(m, d):
        return pltpu.make_async_remote_copy(
            src_ref=eout.at[m, plane_peer(d)],
            dst_ref=ret.at[m, j],
            send_sem=ys.at[m],
            recv_sem=yr.at[m],
            device_id={"tile": plane_peer(d) * ZN + z},
            device_id_type=MESH,
        )

    def all_of(src, dst, m, send_sem, recv_sem):
        return pltpu.make_async_remote_copy(
            src_ref=src.at[m, pl.ds(0, JN - 1)],
            dst_ref=dst.at[m, pl.ds(0, JN - 1)],
            send_sem=send_sem.at[m],
            recv_sem=recv_sem.at[m],
            device_id={"tile": t},
            device_id_type=MESH,
        )

    slots = JN * CAP
    slot_of = lax.broadcasted_iota(jnp.int32, (slots, block), 0).astype(f32)

    def piece_meta(m):
        s, h = piece(m)
        meta = meta_all[s]
        meta = jnp.where(h == 0, meta[:, 0:block], meta[:, block:])
        return meta[0:2] - (z * slots).astype(f32), meta[2:4]

    def stage_dispatch(m):
        s, h = piece(m)
        pos, _ = piece_meta(m)
        table = jnp.where((slot_of == pos[0:1]) | (slot_of == pos[1:2]), 1.0, 0.0).astype(bf16)
        part = pl.ds(pl.multiple_of(h * block, block), block)
        picked = jnp.dot(table, x_all[s, part], preferred_element_type=f32)
        disp[m] = picked.reshape(JN, CAP, model).astype(bf16)

        def start(d, carry):
            dispatch_copy(m, d).start()
            return carry

        lax.fori_loop(1, JN, start, 0)
        recv[m, j] = disp[m, j]

    def stage_expert(m):
        all_of(disp, recv, m, xs, xr).wait_recv()
        zrows = recv[m].astype(f32).reshape(slots, model).astype(bf16)
        gate_part = jnp.dot(zrows, wg[...], preferred_element_type=f32)
        up_part = jnp.dot(zrows, wu[...], preferred_element_type=f32)
        hidden = (gate_part / (1.0 + jnp.exp(-gate_part)) * up_part).astype(bf16)
        result = jnp.dot(hidden, wd[...], preferred_element_type=f32)
        eout[m] = result.reshape(JN, CAP, model).astype(bf16)

        def start(d, carry):
            return_copy(m, d).start()
            return carry

        lax.fori_loop(1, JN, start, 0)
        ret[m, j] = eout[m, j]

    def sum_copy(m, dst, recv_sem, to):
        return pltpu.make_async_remote_copy(
            src_ref=rs_out.at[m],
            dst_ref=dst,
            send_sem=rs_send.at[m],
            recv_sem=recv_sem,
            device_id={"tile": to},
            device_id_type=MESH,
        )

    def to_merge(m, h):
        kind = jnp.where(end, 0, 1)
        return sum_copy(m, merge_in.at[kind, h], merge_recv.at[kind, h], t_in)

    def to_final(m, s, h):
        side = jnp.where(end & ((m == 4) | (m == 5)), 2, jnp.where(z < s, 0, 1))
        return sum_copy(m, final_in.at[side, h], final_recv.at[side, h], j * ZN + s)

    def stage_combine(m):
        all_of(eout, ret, m, ys, yr).wait_recv()
        s, h = piece(m)
        pos, gate = piece_meta(m)
        weights = jnp.where(slot_of == pos[0:1], gate[0:1], 0.0) + jnp.where(
            slot_of == pos[1:2], gate[1:2], 0.0
        )
        part = lax.dot_general(
            weights.astype(bf16),
            ret[m].astype(f32).reshape(slots, model).astype(bf16),
            (((0,), (0,)), ((), ())),
            preferred_element_type=f32,
        )

        @pl.when(m < 2)
        def _():
            own[pl.ds(pl.multiple_of(h * block, block), block)] = part

        @pl.when(end & ((m == 2) | (m == 4) | (m == 5) | (m == 7)))
        def _():
            rs_out[m] = part.astype(bf16)
            to_final(m, s, h).start()

        @pl.when((m == 3) | (end & (m == 6)) | (~end & (m == 5)))
        def _():
            rs_out[m] = part.astype(bf16)
            to_merge(m, h).start()

        @pl.when(~end & (m == 2))
        def _():
            partial[...] = part

        def merge(kind):
            sum_copy(m, merge_in.at[kind, h], merge_recv.at[kind, h], t).wait_recv()
            rs_out[m] = (part + merge_in[kind, h].astype(f32)).astype(bf16)
            to_final(m, s, h).start()

        @pl.when(~end & ((m == 4) | (m == 6)))
        def _():
            merge(1)

        @pl.when(~end & (m == 7))
        def _():
            merge(0)

    def late_merge():
        sum_copy(2, merge_in.at[0, 0], merge_recv.at[0, 0], t).wait_recv()
        rs_out[2] = (partial[...] + merge_in[0, 0].astype(f32)).astype(bf16)
        to_final(2, in1, 0).start()

    for c in early:
        c.wait()
    halo_wait(0)
    attend(0)
    attend(1)
    for c in mid:
        c.wait()
    finish(0)
    own_in(0).start()

    @pl.when(~end)
    def _():
        own_out(0).start()

    for d in range(1, ZN):
        src = lax.rem(z + d, ZN)
        pltpu.make_async_remote_copy(
            src_ref=meta_own,
            dst_ref=meta_all.at[src],
            send_sem=meta_send.at[0],
            recv_sem=meta_recv.at[src],
            device_id={"tile": t},
            device_id_type=MESH,
        ).wait_recv()
    for c in late:
        c.wait()
    halo_wait(1)
    attend(2)
    attend(3)
    finish(1)

    @pl.when(end)
    def _():
        own_in(1).start()

    def step(k, carry):
        arrive(k)

        @pl.when(k < PIECES)
        def _():
            stage_dispatch(k)

        @pl.when((k >= 1) & (k < PIECES + 1))
        def _():
            stage_expert(k - 1)

        @pl.when(k >= 2)
        def _():
            stage_combine(k - 2)

        @pl.when(~end & (k == 7))
        def _():
            late_merge()

        return carry

    lax.fori_loop(0, PIECES + 2, step, 0)

    def add_final(side, h):
        sum_copy(0, final_in.at[side, h], final_recv.at[side, h], t).wait_recv()
        part = slice(h * block, (h + 1) * block)
        own[part] = own[part] + final_in[side, h].astype(f32)

    for h in range(2):

        @pl.when(z > 0)
        def _():
            add_final(0, h)

        @pl.when(z < ZN - 1)
        def _():
            add_final(1, h)

        @pl.when(end)
        def _():
            add_final(2, h)

        part = slice(h * block, (h + 1) * block)
        out_ref[part] = (own[part] + resid[part].astype(f32)).astype(bf16)

    for d in range(1, ZN):
        send_meta(d).wait_send()

    @pl.when(t > 0)
    def _():
        for kv in range(2):
            halo_copy(1, kv).wait_send()

    for h in range(2):
        own_in(h).wait_send()

        @pl.when(~end)
        def _():
            own_out(h).wait_send()
            for slot in (in1, in2, out1):
                forward(slot, h, t_in).wait_send()

    def drain(m, carry):
        all_of(disp, recv, m, xs, xr).wait_send()
        all_of(eout, ret, m, ys, yr).wait_send()

        @pl.when(m >= 2)
        def _():
            sum_copy(m, final_in.at[0, 0], final_recv.at[0, 0], t).wait_send()

        return carry

    lax.fori_loop(0, PIECES, drain, 0)


def local(
    inputs,
    queries,
    key_vectors,
    values,
    out_weight,
    norm_gain,
    routes,
    route_gates,
    w_gate,
    w_up,
    w_down,
):
    rows, model = inputs.shape
    wide = w_gate.shape[2]
    plane = XL * DP
    halo = R_IL * plane
    bf16 = jnp.bfloat16
    f32 = jnp.float32
    vmem = pl.BlockSpec(memory_space=pltpu.VMEM)
    anywhere = pl.BlockSpec(memory_space=pl.ANY)
    dma = pltpu.SemaphoreType.DMA
    return pl.pallas_call(
        layer_kernel,
        out_shape=jax.ShapeDtypeStruct((rows, model), bf16),
        in_specs=[anywhere] * 5 + [vmem] * 3 + [anywhere] * 3,
        out_specs=vmem,
        scratch_shapes=[
            pltpu.VMEM((rows, model), bf16),
            pltpu.VMEM((rows, model), bf16),
            pltpu.VMEM((rows + 2 * halo, model), bf16),
            pltpu.VMEM((rows + 2 * halo, model), bf16),
            pltpu.VMEM((model, model), bf16),
            pltpu.VMEM((rows, model), bf16),
            pltpu.VMEM((4 * plane, (2 * R_IL + 1) * plane), f32),
            pltpu.VMEM((model, wide), bf16),
            pltpu.VMEM((model, wide), bf16),
            pltpu.VMEM((wide, model), bf16),
            pltpu.VMEM((8, rows), f32),
            pltpu.VMEM((ZN, 8, rows), f32),
            pltpu.VMEM((ZN, rows, model), bf16),
            pltpu.VMEM((rows, model), bf16),
            pltpu.VMEM((PIECES, JN, CAP, model), bf16),
            pltpu.VMEM((PIECES, JN, CAP, model), bf16),
            pltpu.VMEM((PIECES, JN, CAP, model), bf16),
            pltpu.VMEM((PIECES, JN, CAP, model), bf16),
            pltpu.VMEM((rows, model), f32),
            pltpu.VMEM((rows // 2, model), f32),
            pltpu.VMEM((PIECES, rows // 2, model), bf16),
            pltpu.VMEM((2, 2, rows // 2, model), bf16),
            pltpu.VMEM((3, 2, rows // 2, model), bf16),
            dma((8,)),
            dma((4,)),
            dma((4,)),
            dma((3,)),
            dma((ZN,)),
            dma((2, 2)),
            dma((ZN, 2)),
            dma((ZN, 2)),
            dma((PIECES,)),
            dma((PIECES,)),
            dma((PIECES,)),
            dma((PIECES,)),
            dma((PIECES,)),
            dma((2, 2)),
            dma((3, 2)),
        ],
        compiler_params=pltpu.CompilerParams(
            collective_id=1, has_side_effects=True, vmem_limit_bytes=58 * 1024 * 1024
        ),
    )(
        inputs,
        queries,
        key_vectors,
        values,
        out_weight,
        norm_gain.reshape(1, model),
        routes.T,
        route_gates.T,
        w_gate,
        w_up,
        w_down,
    )


def solution(mesh):
    return jax.shard_map(
        local,
        mesh=mesh,
        in_specs=(
            P(("rep", "tile"), None),
            P(("rep", "tile"), None),
            P(("rep", "tile"), None),
            P(("rep", "tile"), None),
            P(),
            P(),
            P(("rep", "tile"), None),
            P(("rep", "tile"), None),
            P("tile", None, None),
            P("tile", None, None),
            P("tile", None, None),
        ),
        out_specs=P(("rep", "tile"), None),
        check_vma=False,
    )
```

```python
import jax
import jax.numpy as jnp
from jax import lax
from jax.experimental import pallas as pl
from jax.experimental.pallas import tpu as pltpu
from jax.sharding import PartitionSpec as P

HEADS = 16
HD = 64
IL_DEV = 4
XL = 8
DP = 8
R_IL = 2
R_XL = 2
R_DP = 2
ZN = 4
JN = 16
CAP = 8
PIECES = 2 * ZN
MESH = pl.DeviceIdType.MESH


def layer_kernel(
    x_hbm,
    q_hbm,
    k_hbm,
    v_hbm,
    ow_hbm,
    gain_ref,
    routes_ref,
    gates_ref,
    wg_hbm,
    wu_hbm,
    wd_hbm,
    out_ref,
    x_in,
    q_in,
    ke,
    ve,
    ow,
    att,
    near,
    wg,
    wu,
    wd,
    meta_own,
    meta_all,
    x_all,
    resid,
    disp,
    recv,
    eout,
    ret,
    own,
    partial,
    rs_out,
    merge_in,
    final_in,
    l_sem,
    h_send,
    h_recv,
    meta_send,
    meta_recv,
    ag_send,
    fw_send,
    ag_recv,
    xs,
    xr,
    ys,
    yr,
    rs_send,
    merge_recv,
    final_recv,
):
    t = lax.axis_index("tile")
    tiles = lax.axis_size("tile")
    z = lax.rem(t, ZN)
    j = lax.div(t, ZN)
    rows = x_in.shape[0]
    model = x_in.shape[1]
    plane = XL * DP
    halo = R_IL * plane
    keys = (2 * R_IL + 1) * plane
    bf16 = jnp.bfloat16
    f32 = jnp.float32

    def local_copy(src, dst, n):
        return pltpu.make_async_copy(src, dst, l_sem.at[n])

    early = [
        local_copy(k_hbm, ke.at[pl.ds(halo, rows)], 0),
        local_copy(v_hbm, ve.at[pl.ds(halo, rows)], 1),
        local_copy(q_hbm, q_in, 2),
    ]
    mid = [local_copy(x_hbm, x_in, 3), local_copy(ow_hbm, ow, 4)]
    late = [
        local_copy(wg_hbm.at[0], wg, 5),
        local_copy(wu_hbm.at[0], wu, 6),
        local_copy(wd_hbm.at[0], wd, 7),
    ]

    barrier = pltpu.get_barrier_semaphore()

    def greet(tile):
        pl.semaphore_signal(barrier, inc=1, device_id={"tile": tile}, device_id_type=MESH)

    def z_peer(d):
        return j * ZN + lax.rem(z + d, ZN)

    peers = [lax.rem(j + d, JN) for d in range(JN)]

    @pl.when(t > 0)
    def _():
        greet(t - 1)

    @pl.when(t < tiles - 1)
    def _():
        greet(t + 1)

    for d in range(1, ZN):
        greet(z_peer(d))

    for d in range(1, JN):
        greet(peers[d] * ZN + z)
    for c in early + mid + late:
        c.start()
    pl.semaphore_wait(
        barrier,
        JN - 1 + ZN - 1 + jnp.where(t > 0, 1, 0) + jnp.where(t < tiles - 1, 1, 0),
    )

    def halo_copy(n, kv):
        src, dst = ((rows - halo, 0), (0, halo + rows))[n]
        return pltpu.make_async_remote_copy(
            src_ref=(k_hbm, v_hbm)[kv].at[pl.ds(src, halo)],
            dst_ref=(ke, ve)[kv].at[pl.ds(dst, halo)],
            send_sem=h_send.at[2 * n + kv],
            recv_sem=h_recv.at[2 * n + kv],
            device_id={"tile": t + 1 if n == 0 else t - 1},
            device_id_type=MESH,
        )

    @pl.when(t < tiles - 1)
    def _():
        for kv in range(2):
            halo_copy(0, kv).start()

    @pl.when(t == 0)
    def _():
        ke[0:halo] = jnp.zeros((halo, model), bf16)
        ve[0:halo] = jnp.zeros((halo, model), bf16)

    @pl.when(t == tiles - 1)
    def _():
        ke[halo + rows :] = jnp.zeros((halo, model), bf16)
        ve[halo + rows :] = jnp.zeros((halo, model), bf16)

    def halo_wait(n):
        @pl.when(t > 0 if n == 0 else t < tiles - 1)
        def _():
            for kv in range(2):
                halo_copy(n, kv).wait_recv()

    block = rows // 2
    ti = lax.broadcasted_iota(jnp.int32, (rows, rows), 0)
    tj = lax.broadcasted_iota(jnp.int32, (rows, rows), 1)
    same = ti == tj
    before = (ti < tj) & ((ti < block) == (tj < block))
    route = routes_ref[...].astype(f32)
    cols = [
        jnp.sum(jnp.where(same, route[k : k + 1], 0.0), axis=1, keepdims=True) for k in range(2)
    ]
    for k in range(2):
        r = route[k : k + 1]
        hits = jnp.where(cols[0] == r, 1.0, 0.0) + jnp.where(cols[1] == r, 1.0, 0.0)
        rank = jnp.sum(jnp.where(before, hits, 0.0), axis=0, keepdims=True)
        column = jnp.floor(r * (1.0 / ZN))
        meta_own[k : k + 1, :] = (r - ZN * column) * (JN * CAP) + column * CAP + rank
    meta_own[2:4, :] = gates_ref[...]
    meta_own[4:8, :] = jnp.zeros((4, rows), f32)

    def send_meta(d):
        return pltpu.make_async_remote_copy(
            src_ref=meta_own,
            dst_ref=meta_all.at[z],
            send_sem=meta_send.at[d - 1],
            recv_sem=meta_recv.at[z],
            device_id={"tile": z_peer(d)},
            device_id_type=MESH,
        )

    for d in range(1, ZN):
        send_meta(d).start()
    meta_all[z] = meta_own[...]

    for kv in range(2):

        @pl.when(t < tiles - 1)
        def _():
            halo_copy(0, kv).wait_send()

        @pl.when(t > 0)
        def _():
            halo_copy(1, kv).start()

    qi = lax.rem(lax.broadcasted_iota(jnp.int32, (4 * plane, keys), 0), plane)
    ki = lax.broadcasted_iota(jnp.int32, (4 * plane, keys), 1)
    kp = lax.rem(ki, plane)
    close = (jnp.abs(lax.div(qi, DP) - lax.div(kp, DP)) <= R_XL) & (
        jnp.abs(lax.rem(qi, DP) - lax.rem(kp, DP)) <= R_DP
    )
    near[...] = jnp.where(close, 0.0, -1e30)
    kcol = lax.div(lax.broadcasted_iota(jnp.int32, (1, keys), 1), plane)
    lane_head = lax.div(lax.broadcasted_iota(jnp.int32, (plane, 4 * HD), 1), HD)

    def attend(i):
        outside = ((t == 0) & (kcol < R_IL - i)) | (
            (t == tiles - 1) & (kcol > IL_DEV - 1 + R_IL - i)
        )
        bias = near[...] + jnp.where(outside, -1e30, 0.0)
        for g in range(HEADS // 4):
            lanes = slice(g * 4 * HD, (g + 1) * 4 * HD)
            q4 = q_in[i * plane : (i + 1) * plane, lanes].astype(f32) * (1.0 / HD**0.5)
            stacked = jnp.concatenate(
                [jnp.where(lane_head == h, q4, 0.0).astype(bf16) for h in range(4)], axis=0
            )
            window = slice(i * plane, i * plane + keys)
            scores = lax.dot_general(
                stacked,
                ke[window, lanes],
                (((1,), (1,)), ((), ())),
                preferred_element_type=f32,
            )
            scores = scores + bias
            highest = jnp.max(scores, axis=1, keepdims=True)
            weights = jnp.exp(scores - highest)
            totals = jnp.sum(weights, axis=1, keepdims=True)
            probs = (weights * (1.0 / totals)).astype(bf16)
            mixed = jnp.dot(probs, ve[window, lanes], preferred_element_type=f32)
            picked = mixed[0:plane]
            for h in range(1, 4):
                picked = jnp.where(lane_head == h, mixed[h * plane : (h + 1) * plane], picked)
            att[i * plane : (i + 1) * plane, lanes] = picked.astype(bf16)

    def finish(h):
        part = slice(h * block, (h + 1) * block)
        sums = x_in[part].astype(f32) + jnp.dot(att[part], ow[...], preferred_element_type=f32)
        rounded = sums.astype(bf16)
        wide = rounded.astype(f32)
        mean_square = jnp.mean(wide * wide, axis=1, keepdims=True)
        resid[part] = rounded
        x_all[z, part] = (wide * lax.rsqrt(mean_square + 1e-06) * gain_ref[...]).astype(bf16)

    def tile_copy(slot, h, to, send_sem):
        part = pl.ds(pl.multiple_of(h * block, block), block)
        return pltpu.make_async_remote_copy(
            src_ref=x_all.at[slot, part],
            dst_ref=x_all.at[slot, part],
            send_sem=send_sem,
            recv_sem=ag_recv.at[slot, h],
            device_id={"tile": to},
            device_id_type=MESH,
        )

    end = (z == 0) | (z == ZN - 1)
    inward = jnp.where(z < 2, 1, -1)
    t_in = t + inward
    t_out = jnp.where(end, t, t - inward)
    in1 = z + inward
    in2 = z + 2 * inward
    out1 = jnp.where(end, z, z - inward)

    def own_in(h):
        return tile_copy(z, h, t_in, ag_send.at[0, h])

    def own_out(h):
        return tile_copy(z, h, t_out, ag_send.at[1, h])

    def forward(slot, h, to):
        return tile_copy(slot, h, to, fw_send.at[slot, h])

    def arrived(slot, h):
        tile_copy(slot, h, t_in, ag_send.at[0, h]).wait_recv()

    def piece(m):
        h = jnp.where((m == 1) | (m >= 5), 1, 0)
        at_end = jnp.where(m < 2, 0, jnp.where(m < 5, m - 1, 8 - m))
        at_mid = jnp.where((m == 4) | (m == 6), -1, jnp.where((m == 3) | (m == 5), 2, 1))
        at_mid = jnp.where(m < 2, 0, at_mid)
        return z + inward * jnp.where(end, at_end, at_mid), h

    def arrive(k):
        @pl.when(end & (k >= 2) & (k < PIECES))
        def _():
            slot, h = piece(k)
            arrived(slot, h)

    def pass_on(k):
        @pl.when(~end & (k == 1))
        def _():
            arrived(in1, 0)
            forward(in1, 0, t_out).start()
            arrived(out1, 0)
            forward(out1, 0, t_in).start()

        @pl.when(~end & (k == 2))
        def _():
            arrived(out1, 1)
            forward(out1, 1, t_in).start()
            own_in(1).start()
            arrived(in2, 0)
            forward(in2, 0, t_out).start()

        @pl.when(~end & (k == 3))
        def _():
            arrived(in2, 1)
            forward(in2, 1, t_out).start()

        @pl.when(~end & (k == 4))
        def _():
            arrived(in1, 1)
            forward(in1, 1, t_out).start()
            own_out(1).start()

    def dispatch_copy(m, d):
        return pltpu.make_async_remote_copy(
            src_ref=disp.at[m, peers[d]],
            dst_ref=recv.at[m, j],
            send_sem=xs.at[m],
            recv_sem=xr.at[m],
            device_id={"tile": peers[d] * ZN + z},
            device_id_type=MESH,
        )

    def return_copy(m, d):
        return pltpu.make_async_remote_copy(
            src_ref=eout.at[m, peers[d]],
            dst_ref=ret.at[m, j],
            send_sem=ys.at[m],
            recv_sem=yr.at[m],
            device_id={"tile": peers[d] * ZN + z},
            device_id_type=MESH,
        )

    def all_of(src, dst, m, send_sem, recv_sem):
        return pltpu.make_async_remote_copy(
            src_ref=src.at[m, pl.ds(0, JN - 1)],
            dst_ref=dst.at[m, pl.ds(0, JN - 1)],
            send_sem=send_sem.at[m],
            recv_sem=recv_sem.at[m],
            device_id={"tile": t},
            device_id_type=MESH,
        )

    slots = JN * CAP
    slot_of = lax.broadcasted_iota(jnp.int32, (slots, block), 0).astype(f32)

    def piece_meta(m):
        s, h = piece(m)
        meta = meta_all[s]
        meta = jnp.where(h == 0, meta[:, 0:block], meta[:, block:])
        return meta[0:2] - (z * slots).astype(f32), meta[2:4]

    def stage_dispatch(m):
        s, h = piece(m)
        pos, _ = piece_meta(m)
        table = jnp.where((slot_of == pos[0:1]) | (slot_of == pos[1:2]), 1.0, 0.0).astype(bf16)
        part = pl.ds(pl.multiple_of(h * block, block), block)
        picked = jnp.dot(table, x_all[s, part], preferred_element_type=f32)
        disp[m] = picked.reshape(JN, CAP, model).astype(bf16)

        for d in range(1, JN):
            dispatch_copy(m, d).start()
        recv[m, j] = disp[m, j]

    def stage_expert(m):
        all_of(disp, recv, m, xs, xr).wait_recv()
        zrows = recv[m].astype(f32).reshape(slots, model).astype(bf16)
        gate_part = jnp.dot(zrows, wg[...], preferred_element_type=f32)
        up_part = jnp.dot(zrows, wu[...], preferred_element_type=f32)
        hidden = (gate_part / (1.0 + jnp.exp(-gate_part)) * up_part).astype(bf16)
        result = jnp.dot(hidden, wd[...], preferred_element_type=f32)
        eout[m] = result.reshape(JN, CAP, model).astype(bf16)

        for d in range(1, JN):
            return_copy(m, d).start()
        ret[m, j] = eout[m, j]

    def sum_copy(m, dst, recv_sem, to):
        return pltpu.make_async_remote_copy(
            src_ref=rs_out.at[m],
            dst_ref=dst,
            send_sem=rs_send.at[m],
            recv_sem=recv_sem,
            device_id={"tile": to},
            device_id_type=MESH,
        )

    def to_merge(m, h):
        kind = jnp.where(end, 0, 1)
        return sum_copy(m, merge_in.at[kind, h], merge_recv.at[kind, h], t_in)

    def to_final(m, s, h):
        side = jnp.where(end & ((m == 4) | (m == 5)), 2, jnp.where(z < s, 0, 1))
        return sum_copy(m, final_in.at[side, h], final_recv.at[side, h], j * ZN + s)

    def stage_combine(m):
        all_of(eout, ret, m, ys, yr).wait_recv()
        s, h = piece(m)
        pos, gate = piece_meta(m)
        weights = jnp.where(slot_of == pos[0:1], gate[0:1], 0.0) + jnp.where(
            slot_of == pos[1:2], gate[1:2], 0.0
        )
        part = lax.dot_general(
            weights.astype(bf16),
            ret[m].astype(f32).reshape(slots, model).astype(bf16),
            (((0,), (0,)), ((), ())),
            preferred_element_type=f32,
        )

        @pl.when(m < 2)
        def _():
            own[pl.ds(pl.multiple_of(h * block, block), block)] = part

        @pl.when(end & ((m == 2) | (m == 4) | (m == 5) | (m == 7)))
        def _():
            rs_out[m] = part.astype(bf16)
            to_final(m, s, h).start()

        @pl.when((m == 3) | (end & (m == 6)) | (~end & (m == 5)))
        def _():
            rs_out[m] = part.astype(bf16)
            to_merge(m, h).start()

        @pl.when(~end & (m == 2))
        def _():
            partial[...] = part

        def merge(kind):
            sum_copy(m, merge_in.at[kind, h], merge_recv.at[kind, h], t).wait_recv()
            rs_out[m] = (part + merge_in[kind, h].astype(f32)).astype(bf16)
            to_final(m, s, h).start()

        @pl.when(~end & ((m == 4) | (m == 6)))
        def _():
            merge(1)

        @pl.when(~end & (m == 7))
        def _():
            merge(0)

    def late_merge():
        sum_copy(2, merge_in.at[0, 0], merge_recv.at[0, 0], t).wait_recv()
        rs_out[2] = (partial[...] + merge_in[0, 0].astype(f32)).astype(bf16)
        to_final(2, in1, 0).start()

    for c in early:
        c.wait()
    halo_wait(0)
    attend(0)
    attend(1)
    for c in mid:
        c.wait()
    finish(0)
    own_in(0).start()

    @pl.when(~end)
    def _():
        own_out(0).start()

    for d in range(1, ZN):
        src = lax.rem(z + d, ZN)
        pltpu.make_async_remote_copy(
            src_ref=meta_own,
            dst_ref=meta_all.at[src],
            send_sem=meta_send.at[0],
            recv_sem=meta_recv.at[src],
            device_id={"tile": t},
            device_id_type=MESH,
        ).wait_recv()
    for c in late:
        c.wait()
    halo_wait(1)
    attend(2)
    attend(3)
    finish(1)

    @pl.when(end)
    def _():
        own_in(1).start()

    def step(k, carry):
        arrive(k)

        @pl.when(k < PIECES)
        def _():
            stage_dispatch(k)

        pass_on(k)

        @pl.when((k >= 1) & (k < PIECES + 1))
        def _():
            stage_expert(k - 1)

        @pl.when(k >= 2)
        def _():
            stage_combine(k - 2)

        @pl.when(~end & (k == 7))
        def _():
            late_merge()

        return carry

    lax.fori_loop(0, PIECES + 2, step, 0)

    def add_final(side, h):
        sum_copy(0, final_in.at[side, h], final_recv.at[side, h], t).wait_recv()
        part = slice(h * block, (h + 1) * block)
        own[part] = own[part] + final_in[side, h].astype(f32)

    for h in range(2):

        @pl.when(z > 0)
        def _():
            add_final(0, h)

        @pl.when(z < ZN - 1)
        def _():
            add_final(1, h)

        @pl.when(end)
        def _():
            add_final(2, h)

        part = slice(h * block, (h + 1) * block)
        out_ref[part] = (own[part] + resid[part].astype(f32)).astype(bf16)

    for d in range(1, ZN):
        send_meta(d).wait_send()

    @pl.when(t > 0)
    def _():
        for kv in range(2):
            halo_copy(1, kv).wait_send()

    for h in range(2):
        own_in(h).wait_send()

        @pl.when(~end)
        def _():
            own_out(h).wait_send()
            for slot in (in1, in2, out1):
                forward(slot, h, t_in).wait_send()

    def drain(m, carry):
        all_of(disp, recv, m, xs, xr).wait_send()
        all_of(eout, ret, m, ys, yr).wait_send()

        @pl.when(m >= 2)
        def _():
            sum_copy(m, final_in.at[0, 0], final_recv.at[0, 0], t).wait_send()

        return carry

    lax.fori_loop(0, PIECES, drain, 0)


def local(
    inputs,
    queries,
    key_vectors,
    values,
    out_weight,
    norm_gain,
    routes,
    route_gates,
    w_gate,
    w_up,
    w_down,
):
    rows, model = inputs.shape
    wide = w_gate.shape[2]
    plane = XL * DP
    halo = R_IL * plane
    bf16 = jnp.bfloat16
    f32 = jnp.float32
    vmem = pl.BlockSpec(memory_space=pltpu.VMEM)
    anywhere = pl.BlockSpec(memory_space=pl.ANY)
    dma = pltpu.SemaphoreType.DMA
    return pl.pallas_call(
        layer_kernel,
        out_shape=jax.ShapeDtypeStruct((rows, model), bf16),
        in_specs=[anywhere] * 5 + [vmem] * 3 + [anywhere] * 3,
        out_specs=vmem,
        scratch_shapes=[
            pltpu.VMEM((rows, model), bf16),
            pltpu.VMEM((rows, model), bf16),
            pltpu.VMEM((rows + 2 * halo, model), bf16),
            pltpu.VMEM((rows + 2 * halo, model), bf16),
            pltpu.VMEM((model, model), bf16),
            pltpu.VMEM((rows, model), bf16),
            pltpu.VMEM((4 * plane, (2 * R_IL + 1) * plane), f32),
            pltpu.VMEM((model, wide), bf16),
            pltpu.VMEM((model, wide), bf16),
            pltpu.VMEM((wide, model), bf16),
            pltpu.VMEM((8, rows), f32),
            pltpu.VMEM((ZN, 8, rows), f32),
            pltpu.VMEM((ZN, rows, model), bf16),
            pltpu.VMEM((rows, model), bf16),
            pltpu.VMEM((PIECES, JN, CAP, model), bf16),
            pltpu.VMEM((PIECES, JN, CAP, model), bf16),
            pltpu.VMEM((PIECES, JN, CAP, model), bf16),
            pltpu.VMEM((PIECES, JN, CAP, model), bf16),
            pltpu.VMEM((rows, model), f32),
            pltpu.VMEM((rows // 2, model), f32),
            pltpu.VMEM((PIECES, rows // 2, model), bf16),
            pltpu.VMEM((2, 2, rows // 2, model), bf16),
            pltpu.VMEM((3, 2, rows // 2, model), bf16),
            dma((8,)),
            dma((4,)),
            dma((4,)),
            dma((3,)),
            dma((ZN,)),
            dma((2, 2)),
            dma((ZN, 2)),
            dma((ZN, 2)),
            dma((PIECES,)),
            dma((PIECES,)),
            dma((PIECES,)),
            dma((PIECES,)),
            dma((PIECES,)),
            dma((2, 2)),
            dma((3, 2)),
        ],
        compiler_params=pltpu.CompilerParams(
            collective_id=1, has_side_effects=True, vmem_limit_bytes=58 * 1024 * 1024
        ),
    )(
        inputs,
        queries,
        key_vectors,
        values,
        out_weight,
        norm_gain.reshape(1, model),
        routes.T,
        route_gates.T,
        w_gate,
        w_up,
        w_down,
    )


def solution(mesh):
    return jax.shard_map(
        local,
        mesh=mesh,
        in_specs=(
            P(("rep", "tile"), None),
            P(("rep", "tile"), None),
            P(("rep", "tile"), None),
            P(("rep", "tile"), None),
            P(),
            P(),
            P(("rep", "tile"), None),
            P(("rep", "tile"), None),
            P("tile", None, None),
            P("tile", None, None),
            P("tile", None, None),
        ),
        out_specs=P(("rep", "tile"), None),
        check_vma=False,
    )
```
